32 devices in a mesh: ty: 4 (over y, x), tx: 8 (over z, core).
Axes of the slice: x: 2, y: 2, z: 4, core: 2. Of those that a mesh axis runs over, the one named last changes fastest.
Arguments:
- channel_cube: bfloat16 [256, 512, 128], P(('ty', 'tx'))
- footprint: int32 [32, 8], replicated, may hold values 0 or 1
- kernel_sigmas: int32 [4], replicated, may hold values from 1 to 3, as said below
- spectral_taps: int32 [2, 4], replicated, may hold values from 1 to 5, as said below
Outputs:
- snr_cubes: bfloat16 [4, 512, 128, 256], P(None, 'ty', 'tx')
The draws below stay inside these ranges and needn't reach their ends.
Inputs may be any that keep to these rules, and one draw needn't show every extreme that they name: `kernel_sigmas`: some scale has exactly 3. `spectral_taps`: row 0 holds widths up to 5, row 1 dilations up to 4; some scale has width 5 and dilation 4 together.
All inputs are finite; a program needn't handle non-finite values.
Results may differ from the reference program's by a relative error of at most 0.0077.
Values may be sent and summed in bfloat16 or wider, within the bound.
No kernel may reach another device: no remote copies, remote signals or barrier semaphores. Data moves between devices by JAX's collectives and lax.ppermute only.
A program may use at most 192 MiB of HBM per device.

```python
import jax
import jax.numpy as jnp
from jax import lax

NSC = 4
SMAX = 3
WMAX = 5
DMAX = 4
PT = 16
HALO = 9
PADC = 8
NY = 512
NX = 128
CH = 256
MY = 32
MX = 8


def draw_channel_cube(key, part):
    ramp = jnp.arange(NX).astype(jnp.float32) / NX
    column_scale = 0.3 * jnp.exp(jnp.log(10.0) * ramp)
    row_scale = jnp.exp(jax.random.uniform(jax.random.fold_in(key, 11), (NY,), jnp.float32, jnp.log(0.5), jnp.log(2.0)))
    chan_scale = jnp.exp(jax.random.uniform(jax.random.fold_in(key, 12), (CH,), jnp.float32, jnp.log(0.3), jnp.log(3.0)))
    base = jax.random.normal(jax.random.fold_in(key, 13), (CH, NY, NX), jnp.float32)
    return (base * chan_scale[:, None, None] * row_scale[None, :, None] * column_scale[None, None, :]).astype(jnp.bfloat16)


def draw_kernel_sigmas(key, part):
    values = jax.random.randint(jax.random.fold_in(key, 21), (NSC,), 1, SMAX + 1)
    chosen = jax.random.randint(jax.random.fold_in(key, 22), (), 0, NSC)
    return jnp.where(jnp.arange(NSC) == chosen, SMAX, values).astype(jnp.int32)


def draw_spectral_taps(key, part):
    widths = jax.random.randint(jax.random.fold_in(key, 31), (NSC,), 1, WMAX + 1)
    dilations = jax.random.randint(jax.random.fold_in(key, 32), (NSC,), 1, DMAX + 1)
    chosen = jax.random.randint(jax.random.fold_in(key, 33), (), 0, NSC)
    picked = jnp.arange(NSC) == chosen
    widths = jnp.where(picked, WMAX, widths)
    dilations = jnp.where(picked, DMAX, dilations)
    return jnp.stack([widths, dilations]).astype(jnp.int32)


def touch_ends(result, stream_key, smallest, high):
    longest = result.shape.index(max(result.shape))
    spots = []
    for shift in (0, 1):
        where = [jax.random.randint(jax.random.fold_in(stream_key, axis), (), 0, length) for axis, length in enumerate(result.shape)]
        where[longest] = (where[longest] + shift) % result.shape[longest]
        spots.append(tuple(where))
    return result.at[spots[0]].set(smallest).at[spots[1]].set(high)


def setup_inputs(seed: int = 0) -> dict:
    arg_keys = jax.random.split(jax.random.key(seed), 5)
    channel_cube = draw_channel_cube(jax.random.fold_in(arg_keys[4], 71), 0)
    footprint = touch_ends((jax.random.randint(arg_keys[1], (MY, MX), 0, 4) < 3).astype(jnp.int32), jax.random.fold_in(arg_keys[1], 1), 0, 1)
    kernel_sigmas = draw_kernel_sigmas(jax.random.fold_in(arg_keys[4], 71), 0)
    spectral_taps = draw_spectral_taps(jax.random.fold_in(arg_keys[4], 71), 0)
    return {"channel_cube": channel_cube, "footprint": footprint, "kernel_sigmas": kernel_sigmas, "spectral_taps": spectral_taps}


def gauss_taps(sigma_value):
    offsets = jnp.arange(-HALO, HALO + 1).astype(jnp.float32)
    spread = sigma_value.astype(jnp.float32)
    weights = jnp.exp(-offsets * offsets / (2.0 * spread * spread))
    weights = jnp.where(jnp.abs(offsets) <= 3.0 * spread, weights, jnp.float32(0.0))
    return weights / jnp.sum(weights)

def boxcar(field, width, dilation):
    last = field.ndim - 1
    channels = field.shape[last]
    pads = [(0, 0)] * last + [(PADC, PADC)]
    padded = jnp.pad(field, pads)
    total = jnp.zeros(field.shape, jnp.float32)
    for step in range(WMAX):
        start = (PADC + dilation * (step - (width - 1) // 2)).astype(jnp.int32)
        piece = lax.dynamic_slice_in_dim(padded, start, channels, last)
        total = total + jnp.where(step < width, piece, jnp.float32(0.0))
    return total / width.astype(jnp.float32)

def tap_pass(padded, taps_bf, length, axis):
    shape = list(padded.shape)
    shape[axis] = length

    def add_tap(index, total):
        piece = lax.dynamic_slice_in_dim(padded, index, length, axis).astype(jnp.float32)
        return total + taps_bf[index] * piece
    return lax.fori_loop(0, 2 * HALO + 1, add_tap, jnp.zeros(shape, jnp.float32))

def reference(channel_cube, footprint, kernel_sigmas, spectral_taps):
    pixel_mask = jnp.repeat(jnp.repeat(footprint, PT, 0), PT, 1).astype(jnp.float32)
    masked = jnp.where(pixel_mask[None] > 0.5, channel_cube, jnp.zeros_like(channel_cube))
    count = jnp.maximum(jnp.sum(pixel_mask), jnp.float32(1.0))
    masked_f = masked.astype(jnp.float32)
    squares = lax.optimization_barrier(jnp.sum(masked_f * masked_f, axis=(1, 2)))
    channel_noise = jnp.sqrt(squares / count + 1e-06)
    spectral = jnp.transpose(masked, (1, 2, 0))
    padded = jnp.pad(spectral, ((HALO, HALO), (HALO, HALO), (0, 0)))
    results = []
    for scale_idx in range(NSC):
        taps = gauss_taps(kernel_sigmas[scale_idx])
        taps_bf = taps.astype(jnp.bfloat16).astype(jnp.float32)
        rows_pass = tap_pass(padded, taps_bf, NY, 0).astype(jnp.bfloat16)
        smooth = tap_pass(rows_pass, taps_bf, NX, 1)
        width = spectral_taps[0, scale_idx]
        dilation = spectral_taps[1, scale_idx]
        boxed = boxcar(smooth, width, dilation)
        knorm = jnp.sum(taps * taps) / jnp.sqrt(width.astype(jnp.float32))
        scaled = boxed * pixel_mask[:, :, None] / (channel_noise[None, None, :] * knorm)
        results.append(scaled.astype(jnp.bfloat16))
    return jnp.stack(results)
```

```python
import functools

import jax
import jax.numpy as jnp
import numpy as np
from jax import lax
from jax.experimental import pallas as pl
from jax.experimental.pallas import tpu as pltpu
from jax.sharding import PartitionSpec as P

TILE_Y = 128
TILE_X = 16
NSC = 4
WMAX = 5
PT = 16
HALO = 9
SMAX = 3
LANES = 128
WIN_X = TILE_X + 2 * HALO
PACK = 7
HALO_GROUPS = (0, 10, 18)
GROUPS = TILE_X + 3
SIDE = 11
BF16 = jnp.bfloat16
F32 = jnp.float32
BIG = 3.3895313892515355e38
NT = (((1,), (1,)), ((), ()))


def column_group(x):
    return x + 1 if x < HALO else x + 2


def tap_table():
    offsets = np.arange(-HALO, HALO + 1).astype(np.float32)
    rows = []
    for sigma in range(1, SMAX + 1):
        spread = np.float32(sigma)
        weights = np.exp(-offsets * offsets / (np.float32(2.0) * spread * spread))
        weights = np.where(np.abs(offsets) <= 3.0 * spread, weights, np.float32(0.0)).astype(np.float32)
        rows.append(weights / np.sum(weights, dtype=np.float32))
    return rows


def rounded(value):
    return float(np.asarray(value, np.float32).astype(jnp.bfloat16).astype(np.float32))


def taps_at(diff, taps, sigma):
    total = jnp.zeros(diff.shape, F32)
    for k in range(-3 * sigma, 3 * sigma + 1):
        total = jnp.where(diff == k, F32(rounded(taps[k + HALO])), total)
    return total


def iota(shape, axis):
    return lax.broadcasted_iota(jnp.int32, shape, axis)


def tables_kernel(channels, taps_ref, main_ref, halo_ref, *rest):
    x_refs, box_ref = rest[:SMAX], rest[SMAX]
    taps = tap_table()
    for index in range(SMAX):
        sigma = index + 1
        rows = pl.ds(index * TILE_Y, TILE_Y)
        out_y, lane = iota((TILE_Y, LANES), 0), iota((TILE_Y, LANES), 1)
        main_ref[rows, :] = taps_at(lane - out_y, taps[index], sigma).astype(BF16)
        slot, part = lane // (2 * HALO), lane % (2 * HALO)
        in_y = jnp.where(part < HALO, part - HALO, part - HALO + TILE_Y)
        halo = taps_at(in_y - out_y, taps[index], sigma)
        for member in range(PACK):
            halo_ref[member, rows, :] = jnp.where(slot == member, halo, F32(0.0)).astype(BF16)
        shape = x_refs[index].shape
        row, col = iota(shape, 0), iota(shape, 1)
        weight = taps_at(col // PT - row % TILE_X - 3 * sigma, taps[index], sigma)
        x_refs[index][...] = jnp.where(row // TILE_X == col % PT, weight, F32(0.0)).astype(BF16)
    for scale in range(NSC):
        width, dilation = taps_ref[0, scale], taps_ref[1, scale]
        diff = iota((channels, channels), 0) - iota((channels, channels), 1)
        hit = jnp.zeros((channels, channels), F32)
        for step in range(WMAX):
            offset = jnp.where(step < width, dilation * (step - (width - 1) // 2), channels)
            hit = jnp.where(diff == offset, F32(1.0), hit)
        box_ref[scale] = hit.astype(BF16)


def tables(spectral_taps, channels):
    shapes = [(SMAX * TILE_Y, LANES), (PACK, SMAX * TILE_Y, LANES)]
    shapes += [(PT * TILE_X, (TILE_X + 6 * (i + 1)) * PT) for i in range(SMAX)]
    shapes += [(NSC, channels, channels)]
    return pl.pallas_call(
        functools.partial(tables_kernel, channels),
        out_shape=[jax.ShapeDtypeStruct(s, BF16) for s in shapes],
        in_specs=[pl.BlockSpec(memory_space=pltpu.SMEM)],
        out_specs=[pl.BlockSpec(memory_space=pltpu.VMEM)] * len(shapes),
        cost_estimate=pl.CostEstimate(flops=10**7, bytes_accessed=4 * 10**6, transcendentals=0),
        name="tables",
    )(spectral_taps)


def pack_kernel(cube_ref, mask_ref, out_ref, flat_ref):
    ch, ny, nx = cube_ref.shape
    n_rows, n_cols = ny // TILE_Y, nx // TILE_X
    lane_tile = iota((mask_ref.shape[0], nx), 1) // PT
    wide = jnp.zeros((mask_ref.shape[0], nx), F32)
    for j in range(mask_ref.shape[1]):
        column = jnp.broadcast_to(mask_ref[:, j : j + 1].astype(F32), wide.shape)
        wide = jnp.where(lane_tile == j, column, wide)
    mask = jnp.broadcast_to(wide[:, None, :], (ny // PT, PT, nx)).reshape(ny, nx)
    sums = []
    for c in range(ch):
        plane = jnp.where(mask > 0.5, cube_ref[c].astype(F32), F32(0.0))
        sums.append(jnp.sum(plane * plane, axis=0, keepdims=True))
        flat_ref[:, c * nx : (c + 1) * nx] = plane.astype(BF16)
    squares = jnp.minimum(jnp.sum(jnp.concatenate(sums, axis=0), axis=1, keepdims=True), F32(BIG))
    high = squares.astype(BF16).astype(F32)
    mid = (squares - high).astype(BF16).astype(F32)
    low = squares - high - mid

    x_row, x_col = iota((TILE_X * ch, nx), 0), iota((TILE_X * ch, nx), 1)
    code = (x_col - x_row // ch) * ch + x_row % ch
    blocks = [
        jnp.concatenate([jnp.where(code == t * TILE_X * ch + c, F32(1.0), F32(0.0)).astype(BF16) for c in range(ch)], axis=1)
        for t in range(n_cols)
    ]
    h_rows = len(HALO_GROUPS) * ch
    h_row, h_col = iota((h_rows, nx), 0), iota((h_rows, nx), 1)
    h_hit = jnp.where((h_col % TILE_X) // PACK == h_row // ch, h_col // TILE_X * ch + h_row % ch, -1)
    h_blocks = [
        jnp.concatenate([jnp.where(h_hit == t * ch + c, F32(1.0), F32(0.0)).astype(BF16) for c in range(ch)], axis=1)
        for t in range(n_cols)
    ]
    member = (iota((LANES, ch * nx), 1) % TILE_X) % PACK
    slot = iota((LANES, ch * nx), 0) // (2 * HALO)
    keep = member == slot
    spread_row, spread_col = iota((LANES, 2 * PT), 0), iota((LANES, 2 * PT), 1)
    part = spread_row % (2 * HALO)
    spread = jnp.where((spread_col == part + PT - HALO) & (spread_row < PACK * 2 * HALO), F32(1.0), F32(0.0)).astype(BF16)
    s_row, s_col = iota((h_rows, LANES), 0), iota((h_rows, LANES), 1)
    three = lambda value: jnp.concatenate([jnp.broadcast_to(value, (ch, LANES))] * len(HALO_GROUPS), axis=0)
    extra = jnp.where((s_row < ch) & (s_col == LANES - 2), three(high), F32(0.0))
    extra = jnp.where((s_row < ch) & (s_col == LANES - 1), three(mid), extra)
    extra = jnp.where((s_row >= ch) & (s_row < 2 * ch) & (s_col == LANES - 2), three(low), extra)

    zeros = jnp.zeros((PT, ch * nx), BF16)
    for r in range(n_rows):
        above = flat_ref[r * TILE_Y - PT : r * TILE_Y, :] if r else zeros
        below = flat_ref[(r + 1) * TILE_Y : (r + 1) * TILE_Y + PT, :] if r < n_rows - 1 else zeros
        edge = jnp.concatenate([above, below], axis=0)
        edges = jnp.dot(spread, edge, preferred_element_type=F32)
        edges = jnp.where(keep, edges, F32(0.0)).astype(BF16)
        here = flat_ref[r * TILE_Y : (r + 1) * TILE_Y, :]
        for t in range(n_cols):
            main = lax.dot_general(blocks[t], here, NT, preferred_element_type=F32).astype(BF16)
            halo = (lax.dot_general(h_blocks[t], edges, NT, preferred_element_type=F32) + extra).astype(BF16)
            dest = r * n_cols + t
            base = dest * GROUPS * ch
            cut = HALO * ch
            out_ref[dest, ch : ch + cut, :] = main[:cut]
            out_ref[dest, (HALO_GROUPS[1] + 1) * ch : HALO_GROUPS[2] * ch, :] = main[cut:]
            for index, group in enumerate(HALO_GROUPS):
                out_ref[dest, group * ch : (group + 1) * ch, :] = halo[index * ch : (index + 1) * ch]


def pack(cube, footprint):
    ch, ny, nx = cube.shape
    tiles = (ny // TILE_Y) * (nx // TILE_X)
    return pl.pallas_call(
        pack_kernel,
        out_shape=jax.ShapeDtypeStruct((tiles, GROUPS * ch, LANES), BF16),
        in_specs=[pl.BlockSpec(memory_space=pltpu.VMEM)] * 2,
        out_specs=pl.BlockSpec(memory_space=pltpu.VMEM),
        scratch_shapes=[pltpu.VMEM((ny, ch * nx), BF16)],
        name="pack",
    )(cube, footprint)


def main_kernel(
    sigma_ref, taps_ref, tile_mask_ref, footprint_ref, own_ref, left_ref, right_ref,
    main_ref, halo_ref, *rest,
):
    x_refs, box_ref = rest[:SMAX], rest[SMAX]
    out_ref, rows_ref, scale_ref = rest[SMAX + 1 :]
    senders, _, ch, _ = own_ref.shape
    channels = senders * ch
    part = min(senders, 256 // ch)
    step = pl.program_id(0)

    def load(ref, first, group):
        block = ref[pl.ds(first, part), group].astype(F32)
        return block.reshape(part * ch, LANES).astype(BF16)

    @pl.when(step == 0)
    def _():
        lane = iota((8, 2 * LANES), 1)
        pick = jnp.where((lane >= LANES - 2) & (lane <= LANES) | (lane == 2 * LANES - 2), F32(1.0), F32(0.0))
        pick = jnp.where(lane == LANES, F32(0.0), pick).astype(BF16)
        for first in range(0, senders, part):
            both = jnp.concatenate([load(own_ref, first, HALO_GROUPS[0]), load(own_ref, first, HALO_GROUPS[1])], axis=1)
            squares = lax.dot_general(pick, both, NT, preferred_element_type=F32)
            squares = jnp.where(squares >= F32(BIG), F32(jnp.inf), squares)
            count = jnp.maximum(jnp.sum(footprint_ref[...].astype(F32), keepdims=True) * F32(PT * PT), F32(1.0))
            noise = jnp.sqrt(squares / count + F32(1e-06))
            taps = tap_table()
            for scale in range(NSC):
                width = jnp.full(noise.shape, taps_ref[0, scale], jnp.int32).astype(F32)
                sigma = sigma_ref[scale]
                energy = [F32(float(np.sum(t * t, dtype=np.float32))) for t in taps]
                knorm = jnp.full(noise.shape, energy[0], F32)
                for index in range(1, SMAX):
                    knorm = jnp.where(sigma == index + 1, energy[index], knorm)
                knorm = knorm / jnp.sqrt(width)
                scale_ref[scale, :, first * ch : (first + part) * ch] = F32(1.0) / (noise * knorm * width)

        def y_pass(ref, first, group, halo_group, member, x):
            data = jnp.concatenate([load(ref, first, group), load(ref, first, halo_group)], axis=1)
            band = jnp.concatenate([main_ref[...], halo_ref[member]], axis=1)
            rows = lax.dot_general(band, data, NT, preferred_element_type=F32).astype(BF16)
            rows = rows.reshape(SMAX, TILE_Y // PT, PT, part * ch)
            rows_ref[:, :, x, :, first * ch : (first + part) * ch] = rows

        for first in range(0, senders, part):
            for ref, columns, base, at in (
                (left_ref, range(TILE_X - HALO, TILE_X), column_group(TILE_X - HALO), HALO - TILE_X),
                (own_ref, range(TILE_X), 0, HALO),
                (right_ref, range(HALO), 0, HALO + TILE_X),
            ):
                for x in columns:
                    y_pass(ref, first, column_group(x) - base, HALO_GROUPS[x // PACK] - base, x % PACK, x + at)

    seen = tile_mask_ref[step].astype(F32)
    smooth = []
    for index in range(SMAX):
        reach = 3 * (index + 1)
        slab = rows_ref[index, step, HALO - reach : HALO + TILE_X + reach]
        slab = slab.reshape((TILE_X + 2 * reach) * PT, channels)
        smooth.append(jnp.dot(x_refs[index][...], slab, preferred_element_type=F32))
    for scale in range(NSC):
        sigma = sigma_ref[scale]
        field = smooth[0]
        for index in range(1, SMAX):
            field = jnp.where(sigma == index + 1, smooth[index], field)
        boxed = jnp.dot(field.astype(BF16), box_ref[scale], preferred_element_type=F32)
        scaled = boxed * (scale_ref[scale, 0:1, :] * seen)
        out_ref[scale] = scaled.astype(BF16).reshape(PT, TILE_X, channels)


def finish(kernel_sigmas, spectral_taps, tile_mask, footprint, own, left, right, consts):
    senders, _, ch, _ = own.shape
    channels = senders * ch
    smem = pl.BlockSpec(memory_space=pltpu.SMEM)
    vmem = pl.BlockSpec(memory_space=pltpu.VMEM)
    return pl.pallas_call(
        main_kernel,
        grid=(TILE_Y // PT,),
        out_shape=jax.ShapeDtypeStruct((NSC, TILE_Y, TILE_X, channels), BF16),
        in_specs=[smem] * 3 + [vmem] * (4 + len(consts)),
        out_specs=pl.BlockSpec((NSC, PT, TILE_X, channels), lambda i: (0, i, 0, 0)),
        scratch_shapes=[
            pltpu.VMEM((SMAX, TILE_Y // PT, WIN_X, PT, channels), BF16),
            pltpu.VMEM((NSC, 8, channels), F32),
        ],
        compiler_params=pltpu.CompilerParams(vmem_limit_bytes=60 * 2**20),
        name="finish",
    )(kernel_sigmas, spectral_taps, tile_mask, footprint, own, left, right, *consts)


def local(channel_cube, footprint, kernel_sigmas, spectral_taps):
    n_cols = lax.axis_size("tx")
    ch = channel_cube.shape[0]
    channels = ch * lax.axis_size("ty") * n_cols
    packed = pack(channel_cube, footprint)
    own = lax.all_to_all(packed, ("ty", "tx"), split_axis=0, concat_axis=0, tiled=True)
    consts = tables(spectral_taps, channels)
    tile_rows = TILE_Y // PT
    tile_mask = lax.dynamic_slice(
        footprint, (lax.axis_index("ty") * tile_rows, lax.axis_index("tx") * (TILE_X // PT)), (tile_rows, 1)
    )[:, 0]
    up = [(i, i + 1) for i in range(n_cols - 1)]
    down = [(i + 1, i) for i in range(n_cols - 1)]
    left = lax.ppermute(own[:, (GROUPS - SIDE) * ch :], "tx", up)
    right = lax.ppermute(own[:, : SIDE * ch], "tx", down)
    split = lambda block: block.reshape(block.shape[0], -1, ch, LANES)
    return finish(kernel_sigmas, spectral_taps, tile_mask, footprint, split(own), split(left), split(right), consts)


def solution(mesh):
    placed = (P(("ty", "tx"), None, None), P(), P(), P())
    return jax.shard_map(
        local, mesh=mesh, in_specs=placed, out_specs=P(None, "ty", "tx", None), check_vma=False
    )
```

```python
import functools

import jax
import jax.numpy as jnp
import numpy as np
from jax import lax
from jax.experimental import pallas as pl
from jax.experimental.pallas import tpu as pltpu
from jax.sharding import PartitionSpec as P

TILE_Y = 128
TILE_X = 16
NSC = 4
WMAX = 5
PT = 16
HALO = 9
SMAX = 3
LANES = 128
WIN_X = TILE_X + 2 * HALO
PACK = 7
HALO_GROUPS = (0, 10, 18)
GROUPS = TILE_X + 3
SIDE = 11
SPAN = 4
WIDE = 256
BF16 = jnp.bfloat16
F32 = jnp.float32
BIG = 3.3895313892515355e38
NT = (((1,), (1,)), ((), ()))


def column_group(x):
    return x + 1 if x < HALO else x + 2


def tap_table():
    offsets = np.arange(-HALO, HALO + 1).astype(np.float32)
    rows = []
    for sigma in range(1, SMAX + 1):
        spread = np.float32(sigma)
        weights = np.exp(-offsets * offsets / (np.float32(2.0) * spread * spread))
        weights = np.where(np.abs(offsets) <= 3.0 * spread, weights, np.float32(0.0)).astype(np.float32)
        rows.append(weights / np.sum(weights, dtype=np.float32))
    return rows


def rounded(value):
    return float(np.asarray(value, np.float32).astype(jnp.bfloat16).astype(np.float32))


def taps_at(diff, taps, sigma):
    total = jnp.zeros(diff.shape, F32)
    for k in range(-3 * sigma, 3 * sigma + 1):
        total = jnp.where(diff == k, F32(rounded(taps[k + HALO])), total)
    return total


def margin(channels):
    return 0 if channels <= WIDE else LANES


def in_hbm(x):
    return pltpu.with_memory_space_constraint(x, pltpu.MemorySpace.HBM)


def iota(shape, axis):
    return lax.broadcasted_iota(jnp.int32, shape, axis)


def tables_kernel(channels, taps_ref, main_ref, halo_ref, *rest):
    x_refs, box_ref = rest[:SMAX], rest[SMAX]
    taps = tap_table()
    for index in range(SMAX):
        sigma = index + 1
        rows = pl.ds(index * TILE_Y, TILE_Y)
        out_y, lane = iota((TILE_Y, LANES), 0), iota((TILE_Y, LANES), 1)
        main_ref[rows, :] = taps_at(lane - out_y, taps[index], sigma).astype(BF16)
        slot, part = lane // (2 * HALO), lane % (2 * HALO)
        in_y = jnp.where(part < HALO, part - HALO, part - HALO + TILE_Y)
        halo = taps_at(in_y - out_y, taps[index], sigma)
        for member in range(PACK):
            halo_ref[member, rows, :] = jnp.where(slot == member, halo, F32(0.0)).astype(BF16)
        shape = x_refs[index].shape
        row, col = iota(shape, 0), iota(shape, 1)
        weight = taps_at(col // PT - row % TILE_X - 3 * sigma, taps[index], sigma)
        x_refs[index][...] = jnp.where(row // TILE_X == col % PT, weight, F32(0.0)).astype(BF16)
    for scale in range(NSC):
        width, dilation = taps_ref[0, scale], taps_ref[1, scale]
        shape = box_ref.shape[1:]
        diff = iota(shape, 0) - (shape[0] - shape[1]) // 2 - iota(shape, 1)
        hit = jnp.zeros(shape, F32)
        for step in range(WMAX):
            offset = jnp.where(step < width, dilation * (step - (width - 1) // 2), 2 * channels)
            hit = jnp.where(diff == offset, F32(1.0), hit)
        box_ref[scale] = hit.astype(BF16)


def tables(spectral_taps, channels):
    shapes = [(SMAX * TILE_Y, LANES), (PACK, SMAX * TILE_Y, LANES)]
    shapes += [(PT * TILE_X, (TILE_X + 6 * (i + 1)) * PT) for i in range(SMAX)]
    wide = min(channels, WIDE)
    shapes += [(NSC, wide + 2 * margin(channels), wide)]
    return pl.pallas_call(
        functools.partial(tables_kernel, channels),
        out_shape=[jax.ShapeDtypeStruct(s, BF16) for s in shapes],
        in_specs=[pl.BlockSpec(memory_space=pltpu.SMEM)],
        out_specs=[pl.BlockSpec(memory_space=pltpu.VMEM)] * len(shapes),
        compiler_params=pltpu.CompilerParams(vmem_limit_bytes=16 * 2**20),
        cost_estimate=pl.CostEstimate(flops=10**7, bytes_accessed=4 * 10**6, transcendentals=0),
        name="tables",
    )(spectral_taps)


def pack_kernel(cube_ref, cover_hbm, out_ref, land_ref, cover_ref, flat_ref, perm_ref, pick_ref, edge_ref, sems):
    ch, ny, nx = cube_ref.shape
    n_rows, n_cols = ny // TILE_Y, nx // TILE_X
    copies = [pltpu.make_async_copy(cube_ref.at[c], land_ref.at[c], sems.at[c]) for c in range(ch)]
    cover_copy = pltpu.make_async_copy(cover_hbm, cover_ref, sems.at[ch])
    cover_copy.start()
    for copy in copies:
        copy.start()

    block = TILE_X * ch
    x_row, x_col = iota((block, nx), 0), iota((block, nx), 1)
    code = (x_col - x_row // ch) * ch + x_row % ch
    h_rows = len(HALO_GROUPS) * ch
    h_row, h_col = iota((h_rows, nx), 0), iota((h_rows, nx), 1)
    h_code = jnp.where((h_col % TILE_X) // PACK == h_row // ch, h_col // TILE_X * ch + h_row % ch, -1)
    for t in range(n_cols):
        for c in range(ch):
            lanes = slice(c * nx, (c + 1) * nx)
            perm_ref[t * block : (t + 1) * block, lanes] = jnp.where(code == t * block + c, F32(1.0), F32(0.0)).astype(BF16)
            pick_ref[t * h_rows : (t + 1) * h_rows, lanes] = jnp.where(h_code == t * ch + c, F32(1.0), F32(0.0)).astype(BF16)

    cover_copy.wait()
    tile_x, tile_y = cover_ref.shape
    eye = jnp.where(iota((tile_y, tile_y), 0) == iota((tile_y, tile_y), 1), F32(1.0), F32(0.0)).astype(BF16)
    cover = lax.dot_general(eye, cover_ref[...].astype(F32).astype(BF16), NT, preferred_element_type=F32)
    lane_tile = iota((tile_y, nx), 1) // PT
    wide = jnp.zeros((tile_y, nx), F32)
    for j in range(tile_x):
        wide = jnp.where(lane_tile == j, jnp.broadcast_to(cover[:, j : j + 1], wide.shape), wide)
    mask = jnp.broadcast_to(wide[:, None, :], (tile_y, PT, nx)).reshape(ny, nx) > 0.5
    sums = []
    for c in range(ch):
        copies[c].wait()
        plane = jnp.where(mask, land_ref[c].astype(F32), F32(0.0))
        sums.append(jnp.sum(plane * plane, axis=0, keepdims=True))
        flat_ref[:, c * nx : (c + 1) * nx] = plane.astype(BF16)

    cut = HALO * ch
    for first in range(0, n_rows, 2):
        pair = range(first, min(first + 2, n_rows))
        here = flat_ref[first * TILE_Y : (pair[-1] + 1) * TILE_Y, :]
        main = lax.dot_general(perm_ref[...], here, NT, preferred_element_type=F32).astype(BF16)
        for r in pair:
            lanes = slice((r - first) * TILE_Y, (r - first + 1) * TILE_Y)
            for t in range(n_cols):
                tile = main[t * block : (t + 1) * block, lanes]
                out_ref[r * n_cols + t, ch : ch + cut, :] = tile[:cut]
                out_ref[r * n_cols + t, (HALO_GROUPS[1] + 1) * ch : HALO_GROUPS[2] * ch, :] = tile[cut:]

    squares = jnp.minimum(jnp.sum(jnp.concatenate(sums, axis=0), axis=1, keepdims=True), F32(BIG))
    high = squares.astype(BF16).astype(F32)
    mid = (squares - high).astype(BF16).astype(F32)
    low = squares - high - mid
    keep = (iota((LANES, ch * nx), 1) % TILE_X) % PACK == iota((LANES, ch * nx), 0) // (2 * HALO)
    spread_row, spread_col = iota((LANES, 2 * PT), 0), iota((LANES, 2 * PT), 1)
    part = spread_row % (2 * HALO)
    spread = jnp.where((spread_col == part + PT - HALO) & (spread_row < PACK * 2 * HALO), F32(1.0), F32(0.0)).astype(BF16)
    s_row, s_col = iota((h_rows, LANES), 0), iota((h_rows, LANES), 1)
    three = lambda value: jnp.concatenate([jnp.broadcast_to(value, (ch, LANES))] * len(HALO_GROUPS), axis=0)
    extra = jnp.where((s_row < ch) & (s_col == LANES - 2), three(high), F32(0.0))
    extra = jnp.where((s_row < ch) & (s_col == LANES - 1), three(mid), extra)
    extra = jnp.where((s_row >= ch) & (s_row < 2 * ch) & (s_col == LANES - 2), three(low), extra)
    zeros = jnp.zeros((PT, ch * nx), BF16)
    for r in range(n_rows):
        above = flat_ref[r * TILE_Y - PT : r * TILE_Y, :] if r else zeros
        below = flat_ref[(r + 1) * TILE_Y : (r + 1) * TILE_Y + PT, :] if r < n_rows - 1 else zeros
        edge = jnp.dot(spread, jnp.concatenate([above, below], axis=0), preferred_element_type=F32)
        edge_ref[r * LANES : (r + 1) * LANES, :] = jnp.where(keep, edge, F32(0.0)).astype(BF16)
    halos = lax.dot_general(pick_ref[...], edge_ref[...], NT, preferred_element_type=F32)
    for r in range(n_rows):
        for t in range(n_cols):
            halo = (halos[t * h_rows : (t + 1) * h_rows, r * LANES : (r + 1) * LANES] + extra).astype(BF16)
            for index, group in enumerate(HALO_GROUPS):
                out_ref[r * n_cols + t, group * ch : (group + 1) * ch, :] = halo[index * ch : (index + 1) * ch]


def pack(cube, footprint):
    ch, ny, nx = cube.shape
    n_rows, n_cols = ny // TILE_Y, nx // TILE_X
    h_rows = len(HALO_GROUPS) * ch
    need = 2 * (4 * ch * ny * nx + (n_cols * (TILE_X * ch + h_rows) + n_rows * LANES) * ch * nx)
    return pl.pallas_call(
        pack_kernel,
        out_shape=jax.ShapeDtypeStruct((n_rows * n_cols, GROUPS * ch, LANES), BF16),
        in_specs=[pl.BlockSpec(memory_space=pltpu.MemorySpace.HBM)] * 2,
        out_specs=pl.BlockSpec(memory_space=pltpu.VMEM),
        scratch_shapes=[
            pltpu.VMEM((ch, ny, nx), BF16),
            pltpu.VMEM((nx // PT, ny // PT), jnp.int32),
            pltpu.VMEM((ny, ch * nx), BF16),
            pltpu.VMEM((n_cols * TILE_X * ch, ch * nx), BF16),
            pltpu.VMEM((n_cols * h_rows, ch * nx), BF16),
            pltpu.VMEM((n_rows * LANES, ch * nx), BF16),
            pltpu.SemaphoreType.DMA((ch + 1,)),
        ],
        compiler_params=pltpu.CompilerParams(vmem_limit_bytes=min(need + 12 * 2**20, 62 * 2**20)),
        name="pack",
    )(in_hbm(cube), in_hbm(footprint.T))


def main_kernel(
    sigma_ref, taps_ref, tile_mask_ref, footprint_ref, own_ref, left_ref, right_ref,
    main_ref, halo_ref, *rest,
):
    x_refs, box_ref = rest[:SMAX], rest[SMAX]
    out_ref, rows_ref, scale_ref, stage_ref, sems = rest[SMAX + 1 : SMAX + 6]
    smooth_refs = rest[SMAX + 6 :]
    senders, _, ch, _ = own_ref.shape
    channels = senders * ch
    part = min(senders, WIDE // ch)

    def load(ref, first, group):
        block = ref[pl.ds(first, part), group].astype(F32)
        return block.reshape(part * ch, LANES).astype(BF16)

    lane = iota((8, 2 * LANES), 1)
    pick = jnp.where((lane >= LANES - 2) & (lane <= LANES) | (lane == 2 * LANES - 2), F32(1.0), F32(0.0))
    pick = jnp.where(lane == LANES, F32(0.0), pick).astype(BF16)
    for first in range(0, senders, part):
        both = jnp.concatenate([load(own_ref, first, HALO_GROUPS[0]), load(own_ref, first, HALO_GROUPS[1])], axis=1)
        squares = lax.dot_general(pick, both, NT, preferred_element_type=F32)
        squares = jnp.where(squares >= F32(BIG), F32(jnp.inf), squares)
        count = jnp.maximum(jnp.sum(footprint_ref[...].astype(F32), keepdims=True) * F32(PT * PT), F32(1.0))
        noise = jnp.sqrt(squares / count + F32(1e-06))
        taps = tap_table()
        for scale in range(NSC):
            width = jnp.full(noise.shape, taps_ref[0, scale], jnp.int32).astype(F32)
            sigma = sigma_ref[scale]
            energy = [F32(float(np.sum(t * t, dtype=np.float32))) for t in taps]
            knorm = jnp.full(noise.shape, energy[0], F32)
            for index in range(1, SMAX):
                knorm = jnp.where(sigma == index + 1, energy[index], knorm)
            knorm = knorm / jnp.sqrt(width)
            scale_ref[scale, :, first * ch : (first + part) * ch] = F32(1.0) / (noise * knorm * width)

    def y_pass(ref, first, group, halo_group, member, x):
        data = jnp.concatenate([load(ref, first, group), load(ref, first, halo_group)], axis=1)
        band = jnp.concatenate([main_ref[...], halo_ref[member]], axis=1)
        rows = lax.dot_general(band, data, NT, preferred_element_type=F32).astype(BF16)
        rows = rows.reshape(SMAX, TILE_Y // PT, PT, part * ch)
        rows_ref[:, :, x, :, first * ch : (first + part) * ch] = rows

    for first in range(0, senders, part):
        for ref, columns, base, at in (
            (left_ref, range(TILE_X - HALO, TILE_X), column_group(TILE_X - HALO), HALO - TILE_X),
            (own_ref, range(TILE_X), 0, HALO),
            (right_ref, range(HALO), 0, HALO + TILE_X),
        ):
            for x in columns:
                y_pass(ref, first, column_group(x) - base, HALO_GROUPS[x // PACK] - base, x % PACK, x + at)

    slots, _, tall = stage_ref.shape[:3]
    span, phases = tall // PT, TILE_Y // tall
    wide, edge = min(channels, WIDE), margin(channels)

    def out_copy(phase, slot, scale):
        there = out_ref.at[scale, pl.ds(phase * tall, tall)]
        return pltpu.make_async_copy(stage_ref.at[slot, scale], there, sems.at[slot, scale])

    def x_pass(phase, smooth_ref):
        for kind in range(SMAX):
            reach = 3 * (kind + 1)
            for row in range(span):
                for at in range(0, channels, wide):
                    lanes = slice(at, at + wide)
                    slab = rows_ref[kind, phase * span + row, HALO - reach : HALO + TILE_X + reach, :, lanes]
                    slab = slab.reshape((TILE_X + 2 * reach) * PT, wide)
                    field = jnp.dot(x_refs[kind][...], slab, preferred_element_type=F32)
                    smooth_ref[kind, row, :, lanes] = field.astype(BF16)

    def box_pass(phase, slot, smooth_ref, reused):
        for scale in range(NSC):
            if reused:
                out_copy(phase - slots, slot, scale).wait()
            for row in range(span):
                seen = tile_mask_ref[phase * span + row].astype(F32)
                for at in range(0, channels, wide):
                    lanes, first = slice(at, at + wide), at - edge
                    low, high = max(first, 0), min(at + wide + edge, channels)
                    field = smooth_ref[sigma_ref[scale] - 1, row, :, low:high]
                    boxed = jnp.dot(field, box_ref[scale, low - first : high - first], preferred_element_type=F32)
                    scaled = (boxed * (scale_ref[scale, 0:1, lanes] * seen)).astype(BF16)
                    stage_ref[slot, scale, row * PT : (row + 1) * PT, :, lanes] = scaled.reshape(PT, TILE_X, wide)
            out_copy(phase, slot, scale).start()

    for phase in range(slots):
        x_pass(phase, smooth_refs[phase])
        box_pass(phase, phase, smooth_refs[phase], False)

    def again(phase, carry):
        x_pass(phase, smooth_refs[0])
        box_pass(phase, lax.rem(phase, slots), smooth_refs[0], True)
        return carry

    if phases > slots:
        lax.fori_loop(slots, phases, again, 0)
    for phase in range(phases - slots, phases):
        for scale in range(NSC):
            out_copy(phase, phase % slots, scale).wait()


def finish(kernel_sigmas, spectral_taps, tile_mask, footprint, own, left, right, consts):
    senders, _, ch, _ = own.shape
    channels = senders * ch
    span, slots = (SPAN, TILE_Y // PT // SPAN) if channels <= WIDE else (1, 2)
    need = 2 * channels * (SMAX * TILE_Y * WIN_X + slots * span * (NSC + SMAX) * PT * TILE_X)
    smem = pl.BlockSpec(memory_space=pltpu.SMEM)
    vmem = pl.BlockSpec(memory_space=pltpu.VMEM)
    return pl.pallas_call(
        main_kernel,
        out_shape=jax.ShapeDtypeStruct((NSC, TILE_Y, TILE_X, channels), BF16),
        in_specs=[smem] * 3 + [vmem] * (4 + len(consts)),
        out_specs=pl.BlockSpec(memory_space=pltpu.MemorySpace.HBM),
        scratch_shapes=[
            pltpu.VMEM((SMAX, TILE_Y // PT, WIN_X, PT, channels), BF16),
            pltpu.VMEM((NSC, 8, channels), F32),
            pltpu.VMEM((slots, NSC, span * PT, TILE_X, channels), BF16),
            pltpu.SemaphoreType.DMA((slots, NSC)),
        ]
        + [pltpu.VMEM((SMAX, span, PT * TILE_X, channels), BF16)] * slots,
        compiler_params=pltpu.CompilerParams(vmem_limit_bytes=need + 6 * 2**20 if channels <= WIDE else 62 * 2**20),
        name="finish",
    )(kernel_sigmas, spectral_taps, tile_mask, footprint.T, own, left, right, *consts)


def local(channel_cube, footprint, kernel_sigmas, spectral_taps):
    n_cols = lax.axis_size("tx")
    ch = channel_cube.shape[0]
    channels = ch * lax.axis_size("ty") * n_cols
    packed = pack(channel_cube, footprint)
    own = lax.all_to_all(packed, ("ty", "tx"), split_axis=0, concat_axis=0, tiled=True)
    consts = tables(spectral_taps, channels)
    tile_rows = TILE_Y // PT
    tile_mask = lax.dynamic_slice(
        footprint, (lax.axis_index("ty") * tile_rows, lax.axis_index("tx") * (TILE_X // PT)), (tile_rows, 1)
    )[:, 0]
    up = [(i, i + 1) for i in range(n_cols - 1)]
    down = [(i + 1, i) for i in range(n_cols - 1)]
    left = lax.ppermute(own[:, (GROUPS - SIDE) * ch :], "tx", up)
    right = lax.ppermute(own[:, : SIDE * ch], "tx", down)
    split = lambda block: block.reshape(block.shape[0], -1, ch, LANES)
    return finish(kernel_sigmas, spectral_taps, tile_mask, footprint, split(own), split(left), split(right), consts)


def solution(mesh):
    placed = (P(("ty", "tx"), None, None), P(), P(), P())
    return jax.shard_map(
        local, mesh=mesh, in_specs=placed, out_specs=P(None, "ty", "tx", None), check_vma=False
    )
```

```python
import functools

import jax
import jax.numpy as jnp
import numpy as np
from jax import lax
from jax.experimental import pallas as pl
from jax.experimental.pallas import tpu as pltpu
from jax.sharding import PartitionSpec as P


TILE_Y = 128
TILE_X = 16
NSC = 4
WMAX = 5
PT = 16
HALO = 9
SMAX = 3
LANES = 128
PACK = 7
HALO_GROUPS = (0, 10, 18)
GROUPS = TILE_X + 3
SIDE = 11
SPAN = 4
WIDE = 256
BF16 = jnp.bfloat16
F32 = jnp.float32
BIG = 3.3895313892515355e38
NT = (((1,), (1,)), ((), ()))


def column_group(x):
    return x + 1 if x < HALO else x + 2


def left_column(i):
    x, base = TILE_X - HALO + i, GROUPS - SIDE
    return column_group(x) - base, HALO_GROUPS[x // PACK] - base, x % PACK


def right_column(i):
    return column_group(i), HALO_GROUPS[i // PACK], i % PACK


def odd_tile():
    return lax.rem(lax.axis_index("tx"), 2)


def choose(flag, one, other):
    return jnp.where(flag == 1, jnp.int32(one), jnp.int32(other))


def tap_table():
    offsets = np.arange(-HALO, HALO + 1).astype(np.float32)
    rows = []
    for sigma in range(1, SMAX + 1):
        spread = np.float32(sigma)
        weights = np.exp(-offsets * offsets / (np.float32(2.0) * spread * spread))
        weights = np.where(np.abs(offsets) <= 3.0 * spread, weights, np.float32(0.0)).astype(np.float32)
        rows.append(weights / np.sum(weights, dtype=np.float32))
    return rows


def rounded(value):
    return float(np.asarray(value, np.float32).astype(jnp.bfloat16).astype(np.float32))


def taps_at(diff, taps, sigma):
    total = jnp.zeros(diff.shape, F32)
    for k in range(-3 * sigma, 3 * sigma + 1):
        total = jnp.where(diff == k, F32(rounded(taps[k + HALO])), total)
    return total


def margin(channels):
    return 0 if channels <= WIDE else LANES


def in_hbm(x):
    return pltpu.with_memory_space_constraint(x, pltpu.MemorySpace.HBM)


def iota(shape, axis):
    return lax.broadcasted_iota(jnp.int32, shape, axis)


def tables_kernel(channels, taps_ref, main_ref, halo_ref, *rest):
    x_refs, far_refs, box_ref = rest[:SMAX], rest[SMAX : 2 * SMAX], rest[2 * SMAX]
    odd = odd_tile()
    taps = tap_table()
    for index in range(SMAX):
        sigma = index + 1
        rows = pl.ds(index * TILE_Y, TILE_Y)
        out_y, lane = iota((TILE_Y, LANES), 0), iota((TILE_Y, LANES), 1)
        main_ref[rows, :] = taps_at(lane - out_y, taps[index], sigma).astype(BF16)
        slot, part = lane // (2 * HALO), lane % (2 * HALO)
        in_y = jnp.where(part < HALO, part - HALO, part - HALO + TILE_Y)
        halo = taps_at(in_y - out_y, taps[index], sigma)
        for member in range(PACK):
            halo_ref[member, rows, :] = jnp.where(slot == member, halo, F32(0.0)).astype(BF16)
        reach = 3 * sigma
        for ref, shift in ((x_refs[index], choose(odd, -reach, 0)), (far_refs[index], choose(odd, TILE_X, -reach))):
            row, col = iota(ref.shape, 0), iota(ref.shape, 1)
            weight = taps_at(col // PT - row % TILE_X + shift, taps[index], sigma)
            ref[...] = jnp.where(row // TILE_X == col % PT, weight, F32(0.0)).astype(BF16)
    for scale in range(NSC):
        width, dilation = taps_ref[0, scale], taps_ref[1, scale]
        shape = box_ref.shape[1:]
        diff = iota(shape, 0) - (shape[0] - shape[1]) // 2 - iota(shape, 1)
        hit = jnp.zeros(shape, F32)
        for step in range(WMAX):
            offset = jnp.where(step < width, dilation * (step - (width - 1) // 2), 2 * channels)
            hit = jnp.where(diff == offset, F32(1.0), hit)
        box_ref[scale] = hit.astype(BF16)


def tables(spectral_taps, channels):
    shapes = [(SMAX * TILE_Y, LANES), (PACK, SMAX * TILE_Y, LANES)]
    shapes += [(PT * TILE_X, (TILE_X + 3 * (i + 1)) * PT) for i in range(SMAX)]
    shapes += [(PT * TILE_X, 3 * (i + 1) * PT) for i in range(SMAX)]
    wide = min(channels, WIDE)
    shapes += [(NSC, wide + 2 * margin(channels), wide)]
    return pl.pallas_call(
        functools.partial(tables_kernel, channels),
        out_shape=[jax.ShapeDtypeStruct(s, BF16) for s in shapes],
        in_specs=[pl.BlockSpec(memory_space=pltpu.SMEM)],
        out_specs=[pl.BlockSpec(memory_space=pltpu.VMEM)] * len(shapes),
        compiler_params=pltpu.CompilerParams(vmem_limit_bytes=16 * 2**20),
        cost_estimate=pl.CostEstimate(flops=10**7, bytes_accessed=4 * 10**6, transcendentals=0),
        name="tables",
    )(spectral_taps)


def pack_kernel(cube_ref, cover_hbm, out_ref, land_ref, cover_ref, flat_ref, perm_ref, pick_ref, edge_ref, sems):
    ch, ny, nx = cube_ref.shape
    n_rows, n_cols = ny // TILE_Y, nx // TILE_X
    copies = [pltpu.make_async_copy(cube_ref.at[c], land_ref.at[c], sems.at[c]) for c in range(ch)]
    cover_copy = pltpu.make_async_copy(cover_hbm, cover_ref, sems.at[ch])
    cover_copy.start()
    for copy in copies:
        copy.start()

    block = TILE_X * ch
    x_row, x_col = iota((block, nx), 0), iota((block, nx), 1)
    code = (x_col - x_row // ch) * ch + x_row % ch
    h_rows = len(HALO_GROUPS) * ch
    h_row, h_col = iota((h_rows, nx), 0), iota((h_rows, nx), 1)
    h_code = jnp.where((h_col % TILE_X) // PACK == h_row // ch, h_col // TILE_X * ch + h_row % ch, -1)
    for t in range(n_cols):
        for c in range(ch):
            lanes = slice(c * nx, (c + 1) * nx)
            perm_ref[t * block : (t + 1) * block, lanes] = jnp.where(code == t * block + c, F32(1.0), F32(0.0)).astype(BF16)
            pick_ref[t * h_rows : (t + 1) * h_rows, lanes] = jnp.where(h_code == t * ch + c, F32(1.0), F32(0.0)).astype(BF16)

    cover_copy.wait()
    tile_x, tile_y = cover_ref.shape
    eye = jnp.where(iota((tile_y, tile_y), 0) == iota((tile_y, tile_y), 1), F32(1.0), F32(0.0)).astype(BF16)
    cover = lax.dot_general(eye, cover_ref[...].astype(F32).astype(BF16), NT, preferred_element_type=F32)
    lane_tile = iota((tile_y, nx), 1) // PT
    wide = jnp.zeros((tile_y, nx), F32)
    for j in range(tile_x):
        wide = jnp.where(lane_tile == j, jnp.broadcast_to(cover[:, j : j + 1], wide.shape), wide)
    mask = jnp.broadcast_to(wide[:, None, :], (tile_y, PT, nx)).reshape(ny, nx) > 0.5
    sums = []
    for c in range(ch):
        copies[c].wait()
        plane = jnp.where(mask, land_ref[c].astype(F32), F32(0.0))
        sums.append(jnp.sum(plane * plane, axis=0, keepdims=True))
        flat_ref[:, c * nx : (c + 1) * nx] = plane.astype(BF16)

    cut = HALO * ch
    for first in range(0, n_rows, 2):
        pair = range(first, min(first + 2, n_rows))
        here = flat_ref[first * TILE_Y : (pair[-1] + 1) * TILE_Y, :]
        main = lax.dot_general(perm_ref[...], here, NT, preferred_element_type=F32).astype(BF16)
        for r in pair:
            lanes = slice((r - first) * TILE_Y, (r - first + 1) * TILE_Y)
            for t in range(n_cols):
                tile = main[t * block : (t + 1) * block, lanes]
                out_ref[r * n_cols + t, ch : ch + cut, :] = tile[:cut]
                out_ref[r * n_cols + t, (HALO_GROUPS[1] + 1) * ch : HALO_GROUPS[2] * ch, :] = tile[cut:]

    squares = jnp.minimum(jnp.sum(jnp.concatenate(sums, axis=0), axis=1, keepdims=True), F32(BIG))
    high = squares.astype(BF16).astype(F32)
    mid = (squares - high).astype(BF16).astype(F32)
    low = squares - high - mid
    keep = (iota((LANES, ch * nx), 1) % TILE_X) % PACK == iota((LANES, ch * nx), 0) // (2 * HALO)
    spread_row, spread_col = iota((LANES, 2 * PT), 0), iota((LANES, 2 * PT), 1)
    part = spread_row % (2 * HALO)
    spread = jnp.where((spread_col == part + PT - HALO) & (spread_row < PACK * 2 * HALO), F32(1.0), F32(0.0)).astype(BF16)
    s_row, s_col = iota((h_rows, LANES), 0), iota((h_rows, LANES), 1)
    three = lambda value: jnp.concatenate([jnp.broadcast_to(value, (ch, LANES))] * len(HALO_GROUPS), axis=0)
    extra = jnp.where((s_row < ch) & (s_col == LANES - 2), three(high), F32(0.0))
    extra = jnp.where((s_row < ch) & (s_col == LANES - 1), three(mid), extra)
    extra = jnp.where((s_row >= ch) & (s_row < 2 * ch) & (s_col == LANES - 2), three(low), extra)
    zeros = jnp.zeros((PT, ch * nx), BF16)
    for r in range(n_rows):
        above = flat_ref[r * TILE_Y - PT : r * TILE_Y, :] if r else zeros
        below = flat_ref[(r + 1) * TILE_Y : (r + 1) * TILE_Y + PT, :] if r < n_rows - 1 else zeros
        edge = jnp.dot(spread, jnp.concatenate([above, below], axis=0), preferred_element_type=F32)
        edge_ref[r * LANES : (r + 1) * LANES, :] = jnp.where(keep, edge, F32(0.0)).astype(BF16)
    halos = lax.dot_general(pick_ref[...], edge_ref[...], NT, preferred_element_type=F32)
    for r in range(n_rows):
        for t in range(n_cols):
            halo = (halos[t * h_rows : (t + 1) * h_rows, r * LANES : (r + 1) * LANES] + extra).astype(BF16)
            for index, group in enumerate(HALO_GROUPS):
                out_ref[r * n_cols + t, group * ch : (group + 1) * ch, :] = halo[index * ch : (index + 1) * ch]


def pack(cube, footprint):
    ch, ny, nx = cube.shape
    n_rows, n_cols = ny // TILE_Y, nx // TILE_X
    h_rows = len(HALO_GROUPS) * ch
    need = 2 * (4 * ch * ny * nx + (n_cols * (TILE_X * ch + h_rows) + n_rows * LANES) * ch * nx)
    return pl.pallas_call(
        pack_kernel,
        out_shape=jax.ShapeDtypeStruct((n_rows * n_cols, GROUPS * ch, LANES), BF16),
        in_specs=[pl.BlockSpec(memory_space=pltpu.MemorySpace.HBM)] * 2,
        out_specs=pl.BlockSpec(memory_space=pltpu.VMEM),
        scratch_shapes=[
            pltpu.VMEM((ch, ny, nx), BF16),
            pltpu.VMEM((nx // PT, ny // PT), jnp.int32),
            pltpu.VMEM((ny, ch * nx), BF16),
            pltpu.VMEM((n_cols * TILE_X * ch, ch * nx), BF16),
            pltpu.VMEM((n_cols * h_rows, ch * nx), BF16),
            pltpu.VMEM((n_rows * LANES, ch * nx), BF16),
            pltpu.SemaphoreType.DMA((ch + 1,)),
        ],
        compiler_params=pltpu.CompilerParams(vmem_limit_bytes=min(need + 12 * 2**20, 62 * 2**20)),
        name="pack",
    )(in_hbm(cube), in_hbm(footprint.T))


def cut_kernel(far, own_ref, out_ref):
    odd = odd_tile()
    first = (odd if far else 1 - odd) * (GROUPS - SIDE)
    out_ref[...] = own_ref[:, pl.ds(first, SIDE)]


def cut(own, far):
    senders, _, ch, lanes = own.shape
    return pl.pallas_call(
        functools.partial(cut_kernel, far),
        out_shape=jax.ShapeDtypeStruct((senders, SIDE, ch, lanes), BF16),
        in_specs=[pl.BlockSpec(memory_space=pltpu.VMEM)],
        out_specs=pl.BlockSpec(memory_space=pltpu.VMEM),
        compiler_params=pltpu.CompilerParams(vmem_limit_bytes=6 * 2**20 if senders <= 32 else 24 * 2**20),
        name="cut_far" if far else "cut_near",
    )(own)


def load(ref, first, part, group):
    block = ref[pl.ds(first, part), group].astype(F32)
    return block.reshape(part * ref.shape[2], LANES).astype(BF16)


def y_pass(ref, first, part, group, halo_group, member, main_ref, halo_ref, rows_ref, x):
    data = jnp.concatenate([load(ref, first, part, group), load(ref, first, part, halo_group)], axis=1)
    band = jnp.concatenate([main_ref[...], halo_ref[member]], axis=1)
    rows = lax.dot_general(band, data, NT, preferred_element_type=F32).astype(BF16)
    rows_ref[:, :, x] = rows.reshape(SMAX, TILE_Y // PT, PT, rows.shape[1])


def x_pass(rows_ref, kind, group, start, count, weights_ref):
    slab = rows_ref[kind, group, pl.ds(start, count)]
    slab = slab.reshape(count * PT, slab.shape[-1])
    return jnp.dot(weights_ref[...], slab, preferred_element_type=F32)


def begin_kernel(own_ref, near_ref, main_ref, halo_ref, *rest):
    x_refs, sum_ref, rows_ref = rest[:SMAX], rest[SMAX], rest[SMAX + 1]
    senders, _, ch, _ = own_ref.shape
    part = min(senders, WIDE // ch)
    odd = odd_tile()

    def one(index, carry):
        first = index * part
        passed = functools.partial(y_pass, main_ref=main_ref, halo_ref=halo_ref, rows_ref=rows_ref)
        for i in range(HALO):
            where = [choose(odd, a, b) for a, b in zip(left_column(i), right_column(i))]
            passed(near_ref, first, part, *where, x=choose(odd, i, TILE_X + i))
        for x in range(TILE_X):
            passed(own_ref, first, part, *right_column(x), x=choose(odd, HALO + x, x))
        lanes = pl.ds(pl.multiple_of(first * ch, part * ch), part * ch)
        for group in range(TILE_Y // PT):
            for kind in range(SMAX):
                reach = 3 * (kind + 1)
                start = choose(odd, HALO - reach, 0)
                sum_ref[kind, group, :, lanes] = x_pass(rows_ref, kind, group, start, TILE_X + reach, x_refs[kind])
        return carry

    if senders == part:
        one(0, 0)
    else:
        lax.fori_loop(0, senders // part, one, 0)


def begin(own, near, main, halo, weights):
    senders, _, ch, _ = own.shape
    channels = senders * ch
    wide = min(channels, WIDE)
    rows = (SMAX, TILE_Y // PT, TILE_X + HALO, PT, wide)
    sums = (SMAX, TILE_Y // PT, PT * TILE_X, channels)
    vmem = pl.BlockSpec(memory_space=pltpu.VMEM)
    limit = 2 * int(np.prod(rows)) + 6 * 2**20 if channels <= WIDE else 62 * 2**20
    return pl.pallas_call(
        begin_kernel,
        out_shape=jax.ShapeDtypeStruct(sums, F32),
        in_specs=[vmem] * (4 + len(weights)),
        out_specs=vmem,
        scratch_shapes=[pltpu.VMEM(rows, BF16)],
        compiler_params=pltpu.CompilerParams(vmem_limit_bytes=limit),
        cost_estimate=pl.CostEstimate(flops=10**9, bytes_accessed=8 * 10**6, transcendentals=0),
        name="begin",
    )(own, near, main, halo, *weights)


def finish_kernel(sigma_ref, taps_ref, cover_ref, footprint_ref, own_ref, far_ref, sum_ref, main_ref, halo_ref, *rest):
    far_refs, box_ref, out_ref, rows_ref, scale_ref, stage_ref, sems = rest[:SMAX], *rest[SMAX : SMAX + 6]
    smooth_refs = rest[SMAX + 6 :]
    senders, _, ch, _ = own_ref.shape
    channels = senders * ch
    part = min(senders, WIDE // ch)
    odd = odd_tile()
    tile_x, tile_y = lax.axis_index("tx") * (TILE_X // PT), lax.axis_index("ty") * (TILE_Y // PT)
    slots, _, tall = stage_ref.shape[:3]
    span, phases = tall // PT, TILE_Y // tall
    wide, edge = min(channels, WIDE), margin(channels)

    lane = iota((8, 2 * LANES), 1)
    pick = jnp.where((lane >= LANES - 2) & (lane < LANES) | (lane == 2 * LANES - 2), F32(1.0), F32(0.0)).astype(BF16)
    for first in range(0, senders, part):
        both = jnp.concatenate([load(own_ref, first, part, group) for group in HALO_GROUPS[:2]], axis=1)
        squares = lax.dot_general(pick, both, NT, preferred_element_type=F32)
        squares = jnp.where(squares >= F32(BIG), F32(jnp.inf), squares)
        count = jnp.maximum(jnp.sum(footprint_ref[...].astype(F32), keepdims=True) * F32(PT * PT), F32(1.0))
        noise = jnp.sqrt(squares / count + F32(1e-06))
        energy = [F32(float(np.sum(t * t, dtype=np.float32))) for t in tap_table()]
        for scale in range(NSC):
            width = jnp.full(noise.shape, taps_ref[0, scale], jnp.int32).astype(F32)
            knorm = jnp.full(noise.shape, energy[0], F32)
            for index in range(1, SMAX):
                knorm = jnp.where(sigma_ref[scale] == index + 1, energy[index], knorm)
            knorm = knorm / jnp.sqrt(width)
            scale_ref[scale, :, first * ch : (first + part) * ch] = F32(1.0) / (noise * knorm * width)

    def out_copy(phase, slot, scale):
        there = out_ref.at[scale, pl.ds(phase * tall, tall)]
        return pltpu.make_async_copy(stage_ref.at[slot, scale], there, sems.at[slot, scale])

    def far_y(first):
        for i in range(HALO):
            where = [choose(odd, a, b) for a, b in zip(right_column(i), left_column(i))]
            y_pass(far_ref, first, part, *where, main_ref, halo_ref, rows_ref, i)

    def far_x(first, phase):
        lanes = slice(first * ch, (first + part) * ch)
        for kind in range(SMAX):
            reach = 3 * (kind + 1)
            for row in range(span):
                group = phase * span + row
                added = x_pass(rows_ref, kind, group, choose(odd, 0, HALO - reach), reach, far_refs[kind])
                smooth_refs[phase][kind, row, :, lanes] = (sum_ref[kind, group, :, lanes] + added).astype(BF16)

    def box_pass(phase, slot):
        for scale in range(NSC):
            if phase >= slots:
                out_copy(phase - slots, slot, scale).wait()
            for row in range(span):
                seen = cover_ref[tile_x, tile_y + phase * span + row].astype(F32)
                for at in range(0, channels, wide):
                    lanes, first = slice(at, at + wide), at - edge
                    low, high = max(first, 0), min(at + wide + edge, channels)
                    field = smooth_refs[phase][sigma_ref[scale] - 1, row, :, low:high]
                    boxed = jnp.dot(field, box_ref[scale, low - first : high - first], preferred_element_type=F32)
                    scaled = (boxed * (scale_ref[scale, 0:1, lanes] * seen)).astype(BF16)
                    stage_ref[slot, scale, row * PT : (row + 1) * PT, :, lanes] = scaled.reshape(PT, TILE_X, wide)
            out_copy(phase, slot, scale).start()

    whole = senders == part
    for first in range(0, senders, part):
        far_y(first)
        if not whole:
            for phase in range(phases):
                far_x(first, phase)
    for phase in range(phases):
        if whole:
            far_x(0, phase)
        box_pass(phase, phase % slots)
    for phase in range(phases - slots, phases):
        for scale in range(NSC):
            out_copy(phase, phase % slots, scale).wait()


def finish(kernel_sigmas, spectral_taps, footprint, own, far, sums, main, halo, weights, box):
    senders, _, ch, _ = own.shape
    channels = senders * ch
    wide = min(channels, WIDE)
    span = SPAN if channels <= WIDE else 1
    phases = TILE_Y // PT // span
    rows = (SMAX, TILE_Y // PT, HALO, PT, wide)
    need = 2 * int(np.prod(rows)) + 2 * channels * (2 * span * NSC + SMAX * TILE_Y // PT) * PT * TILE_X
    smem = pl.BlockSpec(memory_space=pltpu.SMEM)
    vmem = pl.BlockSpec(memory_space=pltpu.VMEM)
    return pl.pallas_call(
        finish_kernel,
        out_shape=jax.ShapeDtypeStruct((NSC, TILE_Y, TILE_X, channels), BF16),
        in_specs=[smem] * 3 + [vmem] * (7 + len(weights)),
        out_specs=pl.BlockSpec(memory_space=pltpu.MemorySpace.HBM),
        scratch_shapes=[
            pltpu.VMEM(rows, BF16),
            pltpu.VMEM((NSC, 8, channels), F32),
            pltpu.VMEM((2, NSC, span * PT, TILE_X, channels), BF16),
            pltpu.SemaphoreType.DMA((2, NSC)),
        ]
        + [pltpu.VMEM((SMAX, span, PT * TILE_X, channels), BF16)] * phases,
        compiler_params=pltpu.CompilerParams(
            vmem_limit_bytes=need + 6 * 2**20 if channels <= WIDE else 62 * 2**20
        ),
        name="finish",
    )(kernel_sigmas, spectral_taps, footprint.T, footprint.T, own, far, sums, main, halo, *weights, box)


def local(channel_cube, footprint, kernel_sigmas, spectral_taps):
    n_cols = lax.axis_size("tx")
    ch = channel_cube.shape[0]
    channels = ch * lax.axis_size("ty") * n_cols
    packed = pack(channel_cube, footprint)
    own = lax.all_to_all(packed, ("ty", "tx"), split_axis=0, concat_axis=0, tiled=True)
    own = own.reshape(own.shape[0], GROUPS, ch, LANES)
    far_pairs = [(i, i + 1) for i in range(1, n_cols - 1, 2)]
    near_pairs = [(i, i + 1) for i in range(0, n_cols - 1, 2)]
    both = lambda pairs: pairs + [(j, i) for i, j in pairs]
    far, near = cut(own, True), cut(own, False)
    far = lax.ppermute(far, "tx", both(far_pairs))
    near = lax.ppermute(near, "tx", both(near_pairs))
    main, halo, *weights, box = tables(spectral_taps, channels)
    sums = begin(own, near, main, halo, weights[:SMAX])
    return finish(kernel_sigmas, spectral_taps, footprint, own, far, sums, main, halo, weights[SMAX:], box)


def solution(mesh):
    placed = (P(("ty", "tx"), None, None), P(), P(), P())
    return jax.shard_map(local, mesh=mesh, in_specs=placed, out_specs=P(None, "ty", "tx", None), check_vma=False)
```

```python
import functools

import jax
import jax.numpy as jnp
import numpy as np
from jax import lax
from jax.experimental import pallas as pl
from jax.experimental.pallas import tpu as pltpu
from jax.sharding import PartitionSpec as P


TILE_Y = 128
TILE_X = 16
NSC = 4
WMAX = 5
PT = 16
HALO = 9
SMAX = 3
LANES = 128
TURN = LANES + 8
PACK = 7
HALO_GROUPS = (0, 10, 18)
GROUPS = TILE_X + 3
SIDE = 11
SPAN = 4
WIDE = 256
BF16 = jnp.bfloat16
F32 = jnp.float32
BIG = 3.3895313892515355e38
NT = (((1,), (1,)), ((), ()))


def column_group(x):
    return x + 1 if x < HALO else x + 2


def left_column(i):
    x, base = TILE_X - HALO + i, GROUPS - SIDE
    return column_group(x) - base, HALO_GROUPS[x // PACK] - base, x % PACK


def right_column(i):
    return column_group(i), HALO_GROUPS[i // PACK], i % PACK


def odd_tile():
    return lax.rem(lax.axis_index("tx"), 2)


def choose(flag, one, other):
    return jnp.where(flag == 1, jnp.int32(one), jnp.int32(other))


def tap_table():
    offsets = np.arange(-HALO, HALO + 1).astype(np.float32)
    rows = []
    for sigma in range(1, SMAX + 1):
        spread = np.float32(sigma)
        weights = np.exp(-offsets * offsets / (np.float32(2.0) * spread * spread))
        weights = np.where(np.abs(offsets) <= 3.0 * spread, weights, np.float32(0.0)).astype(np.float32)
        rows.append(weights / np.sum(weights, dtype=np.float32))
    return rows


def rounded(value):
    return float(np.asarray(value, np.float32).astype(jnp.bfloat16).astype(np.float32))


def taps_at(diff, taps, sigma):
    total = jnp.zeros(diff.shape, F32)
    for k in range(-3 * sigma, 3 * sigma + 1):
        total = jnp.where(diff == k, F32(rounded(taps[k + HALO])), total)
    return total


def margin(channels):
    return 0 if channels <= WIDE else LANES


def in_hbm(x):
    return pltpu.with_memory_space_constraint(x, pltpu.MemorySpace.HBM)


def iota(shape, axis):
    return lax.broadcasted_iota(jnp.int32, shape, axis)


def tables_kernel(channels, taps_ref, main_ref, halo_ref, *rest):
    x_refs, far_refs, box_ref = rest[:SMAX], rest[SMAX : 2 * SMAX], rest[2 * SMAX]
    odd = odd_tile()
    taps = tap_table()
    for index in range(SMAX):
        sigma = index + 1
        rows = pl.ds(index * TILE_Y, TILE_Y)
        out_y, lane = iota((TILE_Y, LANES), 0), iota((TILE_Y, LANES), 1)
        main_ref[rows, :] = taps_at(lane - out_y, taps[index], sigma).astype(BF16)
        slot, part = lane // (2 * HALO), lane % (2 * HALO)
        in_y = jnp.where(part < HALO, part - HALO, part - HALO + TILE_Y)
        halo = taps_at(in_y - out_y, taps[index], sigma)
        for member in range(PACK):
            halo_ref[member, rows, :] = jnp.where(slot == member, halo, F32(0.0)).astype(BF16)
        reach = 3 * sigma
        for ref, shift in ((x_refs[index], choose(odd, -reach, 0)), (far_refs[index], choose(odd, TILE_X, -reach))):
            row, col = iota(ref.shape, 0), iota(ref.shape, 1)
            weight = taps_at(col // PT - row % TILE_X + shift, taps[index], sigma)
            ref[...] = jnp.where(row // TILE_X == col % PT, weight, F32(0.0)).astype(BF16)
    for scale in range(NSC):
        width, dilation = taps_ref[0, scale], taps_ref[1, scale]
        shape = box_ref.shape[1:]
        diff = iota(shape, 0) - (shape[0] - shape[1]) // 2 - iota(shape, 1)
        hit = jnp.zeros(shape, F32)
        for step in range(WMAX):
            offset = jnp.where(step < width, dilation * (step - (width - 1) // 2), 2 * channels)
            hit = jnp.where(diff == offset, F32(1.0), hit)
        box_ref[scale] = hit.astype(BF16)


def tables(spectral_taps, channels):
    shapes = [(SMAX * TILE_Y, LANES), (PACK, SMAX * TILE_Y, LANES)]
    shapes += [(PT * TILE_X, (TILE_X + 3 * (i + 1)) * PT) for i in range(SMAX)]
    shapes += [(PT * TILE_X, 3 * (i + 1) * PT) for i in range(SMAX)]
    wide = min(channels, WIDE)
    shapes += [(NSC, wide + 2 * margin(channels), wide)]
    return pl.pallas_call(
        functools.partial(tables_kernel, channels),
        out_shape=[jax.ShapeDtypeStruct(s, BF16) for s in shapes],
        in_specs=[pl.BlockSpec(memory_space=pltpu.SMEM)],
        out_specs=[pl.BlockSpec(memory_space=pltpu.VMEM)] * len(shapes),
        compiler_params=pltpu.CompilerParams(vmem_limit_bytes=16 * 2**20),
        cost_estimate=pl.CostEstimate(flops=10**7, bytes_accessed=4 * 10**6, transcendentals=0),
        name="tables",
    )(spectral_taps)


def pack_kernel(cube_ref, cover_hbm, out_ref, land_ref, cover_ref, flat_ref, turned_ref, sums_ref, pick_ref, edge_ref, sems):
    ch, ny, nx = cube_ref.shape
    n_rows, spans = ny // TILE_Y, nx // LANES
    n_cols, tiles = nx // TILE_X, LANES // TILE_X
    copies = [pltpu.make_async_copy(cube_ref.at[c], land_ref.at[c], sems.at[c]) for c in range(ch)]
    cover_copy = pltpu.make_async_copy(cover_hbm, cover_ref, sems.at[ch])
    cover_copy.start()
    for copy in copies:
        copy.start()

    h_rows = len(HALO_GROUPS) * ch
    h_row, h_col = iota((h_rows, LANES), 0), iota((h_rows, LANES), 1)
    h_code = jnp.where((h_col % TILE_X) // PACK == h_row // ch, h_col // TILE_X * ch + h_row % ch, -1)
    for t in range(tiles):
        for c in range(ch):
            hit = jnp.where(h_code == t * ch + c, F32(1.0), F32(0.0)).astype(BF16)
            pick_ref[t * h_rows : (t + 1) * h_rows, c * LANES : (c + 1) * LANES] = hit
    sums_ref[...] = jnp.zeros(sums_ref.shape, F32)

    cover_copy.wait()
    tile_x, tile_y = cover_ref.shape
    eye = jnp.where(iota((tile_y, tile_y), 0) == iota((tile_y, tile_y), 1), F32(1.0), F32(0.0)).astype(BF16)
    cover = lax.dot_general(eye, cover_ref[...].astype(F32).astype(BF16), NT, preferred_element_type=F32).astype(BF16)

    def transpose(span, wait):
        at = span * LANES if isinstance(span, int) else pl.multiple_of(span * LANES, LANES)
        widen = jnp.where(iota((tile_x, LANES), 0) == span * tiles + iota((tile_x, LANES), 1) // PT, F32(1.0), F32(0.0))
        wide = jnp.dot(cover, widen.astype(BF16), preferred_element_type=F32)
        mask = jnp.broadcast_to(wide[:, None, :], (tile_y, PT, LANES)).reshape(ny, LANES) > 0.5
        for c in range(ch):
            if wait:
                copies[c].wait()
            plane = jnp.where(mask, land_ref[c, :, pl.ds(at, LANES)].astype(F32), F32(0.0))
            sums_ref[c : c + 1, :] += jnp.sum(plane * plane, axis=0, keepdims=True)
            flat_ref[span, :, c * LANES : (c + 1) * LANES] = plane.astype(BF16)
            turned = plane.T
            for r in range(n_rows):
                turned_ref[r, c * TURN : c * TURN + LANES, :] = turned[:, r * TILE_Y : (r + 1) * TILE_Y]
        for x in range(LANES):
            group = column_group(x % TILE_X)
            for r in range(n_rows):
                dest = r * n_cols + span * tiles + x // TILE_X
                column = turned_ref[r, pl.ds(x, ch, stride=TURN), :]
                out_ref[dest, group * ch : (group + 1) * ch, :] = column.astype(BF16)

    if spans == 1:
        transpose(0, True)
    else:
        for copy in copies:
            copy.wait()
        lax.fori_loop(0, spans, lambda span, carry: (transpose(span, False), carry)[1], 0)

    squares = jnp.minimum(jnp.sum(sums_ref[...], axis=1, keepdims=True), F32(BIG))
    high = squares.astype(BF16).astype(F32)
    mid = (squares - high).astype(BF16).astype(F32)
    low = squares - high - mid
    keep = (iota((LANES, ch * LANES), 1) % TILE_X) % PACK == iota((LANES, ch * LANES), 0) // (2 * HALO)
    spread_row, spread_col = iota((LANES, 2 * PT), 0), iota((LANES, 2 * PT), 1)
    part = spread_row % (2 * HALO)
    spread = jnp.where((spread_col == part + PT - HALO) & (spread_row < PACK * 2 * HALO), F32(1.0), F32(0.0)).astype(BF16)
    s_row, s_col = iota((h_rows, LANES), 0), iota((h_rows, LANES), 1)
    three = lambda value: jnp.concatenate([jnp.broadcast_to(value, (ch, LANES))] * len(HALO_GROUPS), axis=0)
    extra = jnp.where((s_row < ch) & (s_col == LANES - 2), three(high), F32(0.0))
    extra = jnp.where((s_row < ch) & (s_col == LANES - 1), three(mid), extra)
    extra = jnp.where((s_row >= ch) & (s_row < 2 * ch) & (s_col == LANES - 2), three(low), extra)
    zeros = jnp.zeros((PT, ch * LANES), BF16)

    def halos(span):
        for r in range(n_rows):
            above = flat_ref[span, r * TILE_Y - PT : r * TILE_Y, :] if r else zeros
            below = flat_ref[span, (r + 1) * TILE_Y : (r + 1) * TILE_Y + PT, :] if r < n_rows - 1 else zeros
            edge = jnp.dot(spread, jnp.concatenate([above, below], axis=0), preferred_element_type=F32)
            edge_ref[r * LANES : (r + 1) * LANES, :] = jnp.where(keep, edge, F32(0.0)).astype(BF16)
        packed = lax.dot_general(pick_ref[...], edge_ref[...], NT, preferred_element_type=F32)
        for r in range(n_rows):
            for t in range(tiles):
                halo = (packed[t * h_rows : (t + 1) * h_rows, r * LANES : (r + 1) * LANES] + extra).astype(BF16)
                for index, group in enumerate(HALO_GROUPS):
                    rows = halo[index * ch : (index + 1) * ch]
                    out_ref[r * n_cols + span * tiles + t, group * ch : (group + 1) * ch, :] = rows

    if spans == 1:
        halos(0)
    else:
        lax.fori_loop(0, spans, lambda span, carry: (halos(span), carry)[1], 0)


def pack(cube, footprint):
    ch, ny, nx = cube.shape
    n_rows, n_cols, spans = ny // TILE_Y, nx // TILE_X, nx // LANES
    h_rows = len(HALO_GROUPS) * ch * (LANES // TILE_X)
    need = 2 * ch * (3 * ny * nx + (2 * ny + h_rows + n_rows * LANES) * LANES)
    return pl.pallas_call(
        pack_kernel,
        out_shape=jax.ShapeDtypeStruct((n_rows * n_cols, GROUPS * ch, LANES), BF16),
        in_specs=[pl.BlockSpec(memory_space=pltpu.MemorySpace.HBM)] * 2,
        out_specs=pl.BlockSpec(memory_space=pltpu.VMEM),
        scratch_shapes=[
            pltpu.VMEM((ch, ny, nx), BF16),
            pltpu.VMEM((nx // PT, ny // PT), jnp.int32),
            pltpu.VMEM((spans, ny, ch * LANES), BF16),
            pltpu.VMEM((n_rows, ch * TURN, TILE_Y), F32),
            pltpu.VMEM((ch, LANES), F32),
            pltpu.VMEM((h_rows, ch * LANES), BF16),
            pltpu.VMEM((n_rows * LANES, ch * LANES), BF16),
            pltpu.SemaphoreType.DMA((ch + 1,)),
        ],
        compiler_params=pltpu.CompilerParams(vmem_limit_bytes=min(need + 12 * 2**20, 62 * 2**20)),
        name="pack",
    )(in_hbm(cube), in_hbm(footprint.T))


def cut_kernel(far, own_ref, out_ref):
    odd = odd_tile()
    first = (odd if far else 1 - odd) * (GROUPS - SIDE)
    out_ref[...] = own_ref[:, pl.ds(first, SIDE)]


def cut(own, far):
    senders, _, ch, lanes = own.shape
    return pl.pallas_call(
        functools.partial(cut_kernel, far),
        out_shape=jax.ShapeDtypeStruct((senders, SIDE, ch, lanes), BF16),
        in_specs=[pl.BlockSpec(memory_space=pltpu.VMEM)],
        out_specs=pl.BlockSpec(memory_space=pltpu.VMEM),
        compiler_params=pltpu.CompilerParams(vmem_limit_bytes=6 * 2**20 if senders <= 32 else 24 * 2**20),
        name="cut_far" if far else "cut_near",
    )(own)


def load(ref, first, part, group):
    block = ref[pl.ds(first, part), group].astype(F32)
    return block.reshape(part * ref.shape[2], LANES).astype(BF16)


def y_pass(ref, first, part, group, halo_group, member, main_ref, halo_ref, rows_ref, x):
    data = jnp.concatenate([load(ref, first, part, group), load(ref, first, part, halo_group)], axis=1)
    band = jnp.concatenate([main_ref[...], halo_ref[member]], axis=1)
    rows = lax.dot_general(band, data, NT, preferred_element_type=F32).astype(BF16)
    rows_ref[:, :, x] = rows.reshape(SMAX, TILE_Y // PT, PT, rows.shape[1])


def x_pass(rows_ref, kind, group, start, count, weights_ref):
    slab = rows_ref[kind, group, pl.ds(start, count)]
    slab = slab.reshape(count * PT, slab.shape[-1])
    return jnp.dot(weights_ref[...], slab, preferred_element_type=F32)


def scale_rows(sigma_ref, taps_ref, cover_ref, footprint_ref, own_ref, first, part):
    lane = iota((8, 2 * LANES), 1)
    pick = jnp.where((lane >= LANES - 2) & (lane < LANES) | (lane == 2 * LANES - 2), F32(1.0), F32(0.0)).astype(BF16)
    both = jnp.concatenate([load(own_ref, first, part, group) for group in HALO_GROUPS[:2]], axis=1)
    squares = lax.dot_general(pick, both, NT, preferred_element_type=F32)
    squares = jnp.where(squares >= F32(BIG), F32(jnp.inf), squares)
    count = jnp.maximum(jnp.sum(footprint_ref[...].astype(F32), keepdims=True) * F32(PT * PT), F32(1.0))
    noise = jnp.sqrt(squares / count + F32(1e-06))
    tile_x, tile_y = lax.axis_index("tx") * (TILE_X // PT), lax.axis_index("ty") * (TILE_Y // PT)
    seen = jnp.zeros(noise.shape, F32)
    for group in range(TILE_Y // PT):
        seen = jnp.where(iota(noise.shape, 0) == group, cover_ref[tile_x, tile_y + group].astype(F32), seen)
    energy = [F32(float(np.sum(t * t, dtype=np.float32))) for t in tap_table()]
    for scale in range(NSC):
        width = jnp.full(noise.shape, taps_ref[0, scale], jnp.int32).astype(F32)
        knorm = jnp.full(noise.shape, energy[0], F32)
        for index in range(1, SMAX):
            knorm = jnp.where(sigma_ref[scale] == index + 1, energy[index], knorm)
        yield scale, seen / (noise * (knorm / jnp.sqrt(width)) * width)


def begin_kernel(sigma_ref, taps_ref, cover_ref, footprint_ref, own_ref, near_ref, main_ref, halo_ref, *rest):
    x_refs, sum_ref, scale_ref, rows_ref = rest[:SMAX], *rest[SMAX : SMAX + 3]
    senders, _, ch, _ = own_ref.shape
    part = min(senders, WIDE // ch)
    odd = odd_tile()

    def one(index, carry):
        first = index * part
        passed = functools.partial(y_pass, main_ref=main_ref, halo_ref=halo_ref, rows_ref=rows_ref)
        for i in range(HALO):
            where = [choose(odd, a, b) for a, b in zip(left_column(i), right_column(i))]
            passed(near_ref, first, part, *where, x=choose(odd, i, TILE_X + i))
        for x in range(TILE_X):
            passed(own_ref, first, part, *right_column(x), x=choose(odd, HALO + x, x))
        lanes = pl.ds(pl.multiple_of(first * ch, part * ch), part * ch)
        for scale, value in scale_rows(sigma_ref, taps_ref, cover_ref, footprint_ref, own_ref, first, part):
            scale_ref[scale, :, lanes] = value
        for group in range(TILE_Y // PT):
            for kind in range(SMAX):
                reach = 3 * (kind + 1)
                start = choose(odd, HALO - reach, 0)
                sum_ref[kind, group, :, lanes] = x_pass(rows_ref, kind, group, start, TILE_X + reach, x_refs[kind])
        return carry

    if senders == part:
        one(0, 0)
    else:
        lax.fori_loop(0, senders // part, one, 0)


def begin(kernel_sigmas, spectral_taps, footprint, own, near, main, halo, weights):
    senders, _, ch, _ = own.shape
    channels = senders * ch
    wide = min(channels, WIDE)
    rows = (SMAX, TILE_Y // PT, TILE_X + HALO, PT, wide)
    sums = (SMAX, TILE_Y // PT, PT * TILE_X, channels)
    smem = pl.BlockSpec(memory_space=pltpu.SMEM)
    vmem = pl.BlockSpec(memory_space=pltpu.VMEM)
    limit = 2 * int(np.prod(rows)) + 6 * 2**20 if channels <= WIDE else 62 * 2**20
    return pl.pallas_call(
        begin_kernel,
        out_shape=[jax.ShapeDtypeStruct(sums, F32), jax.ShapeDtypeStruct((NSC, TILE_Y // PT, channels), F32)],
        in_specs=[smem] * 3 + [vmem] * (5 + len(weights)),
        out_specs=[vmem] * 2,
        scratch_shapes=[pltpu.VMEM(rows, BF16)],
        compiler_params=pltpu.CompilerParams(vmem_limit_bytes=limit),
        cost_estimate=pl.CostEstimate(flops=10**9, bytes_accessed=8 * 10**6, transcendentals=0),
        name="begin",
    )(kernel_sigmas, spectral_taps, footprint.T, footprint.T, own, near, main, halo, *weights)


def finish_kernel(sigma_ref, far_ref, sum_ref, scale_ref, main_ref, halo_ref, *rest):
    far_refs, box_ref, out_ref, rows_ref, stage_ref, sems = rest[:SMAX], *rest[SMAX : SMAX + 5]
    smooth_refs = rest[SMAX + 5 :]
    senders, _, ch, _ = far_ref.shape
    channels = senders * ch
    part = min(senders, WIDE // ch)
    odd = odd_tile()
    slots, _, tall = stage_ref.shape[:3]
    span, phases = tall // PT, TILE_Y // tall
    wide, edge = min(channels, WIDE), margin(channels)

    def out_copy(phase, slot, scale):
        there = out_ref.at[scale, pl.ds(phase * tall, tall)]
        return pltpu.make_async_copy(stage_ref.at[slot, scale], there, sems.at[slot, scale])

    def far_y(first):
        for i in range(HALO):
            where = [choose(odd, a, b) for a, b in zip(right_column(i), left_column(i))]
            y_pass(far_ref, first, part, *where, main_ref, halo_ref, rows_ref, i)

    def far_x(first, phase):
        lanes = slice(first * ch, (first + part) * ch)
        for kind in range(SMAX):
            reach = 3 * (kind + 1)
            for row in range(span):
                group = phase * span + row
                added = x_pass(rows_ref, kind, group, choose(odd, 0, HALO - reach), reach, far_refs[kind])
                smooth_refs[phase][kind, row, :, lanes] = (sum_ref[kind, group, :, lanes] + added).astype(BF16)

    def box_pass(phase, slot):
        for scale in range(NSC):
            if phase >= slots:
                out_copy(phase - slots, slot, scale).wait()
            for row in range(span):
                group = phase * span + row
                for at in range(0, channels, wide):
                    lanes, first = slice(at, at + wide), at - edge
                    low, high = max(first, 0), min(at + wide + edge, channels)
                    field = smooth_refs[phase][sigma_ref[scale] - 1, row, :, low:high]
                    boxed = jnp.dot(field, box_ref[scale, low - first : high - first], preferred_element_type=F32)
                    scaled = (boxed * scale_ref[scale, group : group + 1, lanes]).astype(BF16)
                    stage_ref[slot, scale, row * PT : (row + 1) * PT, :, lanes] = scaled.reshape(PT, TILE_X, wide)
            out_copy(phase, slot, scale).start()

    whole = senders == part
    for first in range(0, senders, part):
        far_y(first)
        if not whole:
            for phase in range(phases):
                far_x(first, phase)
    for phase in range(phases):
        if whole:
            far_x(0, phase)
        box_pass(phase, phase % slots)
    for phase in range(phases - slots, phases):
        for scale in range(NSC):
            out_copy(phase, phase % slots, scale).wait()


def finish(kernel_sigmas, far, sums, scales, main, halo, weights, box):
    senders, _, ch, _ = far.shape
    channels = senders * ch
    wide = min(channels, WIDE)
    span = SPAN if channels <= WIDE else 1
    phases = TILE_Y // PT // span
    slots = min(2, phases)
    rows = (SMAX, TILE_Y // PT, HALO, PT, wide)
    need = 2 * int(np.prod(rows)) + 2 * channels * (slots * span * NSC + SMAX * TILE_Y // PT) * PT * TILE_X
    vmem = pl.BlockSpec(memory_space=pltpu.VMEM)
    return pl.pallas_call(
        finish_kernel,
        out_shape=jax.ShapeDtypeStruct((NSC, TILE_Y, TILE_X, channels), BF16),
        in_specs=[pl.BlockSpec(memory_space=pltpu.SMEM)] + [vmem] * (6 + len(weights)),
        out_specs=pl.BlockSpec(memory_space=pltpu.MemorySpace.HBM),
        scratch_shapes=[
            pltpu.VMEM(rows, BF16),
            pltpu.VMEM((slots, NSC, span * PT, TILE_X, channels), BF16),
            pltpu.SemaphoreType.DMA((slots, NSC)),
        ]
        + [pltpu.VMEM((SMAX, span, PT * TILE_X, channels), BF16)] * phases,
        compiler_params=pltpu.CompilerParams(
            vmem_limit_bytes=need + 6 * 2**20 if channels <= WIDE else 62 * 2**20
        ),
        name="finish",
    )(kernel_sigmas, far, sums, scales, main, halo, *weights, box)


def local(channel_cube, footprint, kernel_sigmas, spectral_taps):
    n_cols = lax.axis_size("tx")
    ch = channel_cube.shape[0]
    channels = ch * lax.axis_size("ty") * n_cols
    packed = pack(channel_cube, footprint)
    own = lax.all_to_all(packed, ("ty", "tx"), split_axis=0, concat_axis=0, tiled=True)
    own = own.reshape(own.shape[0], GROUPS, ch, LANES)
    far_pairs = [(i, i + 1) for i in range(1, n_cols - 1, 2)]
    near_pairs = [(i, i + 1) for i in range(0, n_cols - 1, 2)]
    both = lambda pairs: pairs + [(j, i) for i, j in pairs]
    far, near = cut(own, True), cut(own, False)
    far = lax.ppermute(far, "tx", both(far_pairs))
    near = lax.ppermute(near, "tx", both(near_pairs))
    main, halo, *weights, box = tables(spectral_taps, channels)
    sums, scales = begin(kernel_sigmas, spectral_taps, footprint, own, near, main, halo, weights[:SMAX])
    return finish(kernel_sigmas, far, sums, scales, main, halo, weights[SMAX:], box)


def solution(mesh):
    placed = (P(("ty", "tx"), None, None), P(), P(), P())
    return jax.shard_map(local, mesh=mesh, in_specs=placed, out_specs=P(None, "ty", "tx", None), check_vma=False)
```

```python
import functools

import jax
import jax.numpy as jnp
import numpy as np
from jax import lax
from jax.experimental import pallas as pl
from jax.experimental.pallas import tpu as pltpu
from jax.sharding import PartitionSpec as P


TILE_Y = 128
TILE_X = 16
HALF = TILE_X // 2
NSC = 4
WMAX = 5
PT = 16
HALO = 9
SMAX = 3
LANES = 128
TURN = LANES + 8
PACK = 7
HALO_GROUPS = (0, 10, 18)
GROUPS = TILE_X + 3
SIDE = 11
SPAN = 4
WIDE = 256
BF16 = jnp.bfloat16
F32 = jnp.float32
BIG = 3.3895313892515355e38
NT = (((1,), (1,)), ((), ()))


def column_group(x):
    return x + 1 if x < HALO else x + 2


def left_column(i):
    x, base = TILE_X - HALO + i, GROUPS - SIDE
    return column_group(x) - base, HALO_GROUPS[x // PACK] - base, x % PACK


def right_column(i):
    return column_group(i), HALO_GROUPS[i // PACK], i % PACK


def odd_tile():
    return lax.rem(lax.axis_index("tx"), 2)


def choose(flag, one, other):
    return jnp.where(flag == 1, jnp.int32(one), jnp.int32(other))


def tap_table():
    offsets = np.arange(-HALO, HALO + 1).astype(np.float32)
    rows = []
    for sigma in range(1, SMAX + 1):
        spread = np.float32(sigma)
        weights = np.exp(-offsets * offsets / (np.float32(2.0) * spread * spread))
        weights = np.where(np.abs(offsets) <= 3.0 * spread, weights, np.float32(0.0)).astype(np.float32)
        rows.append(weights / np.sum(weights, dtype=np.float32))
    return rows


def rounded(value):
    return float(np.asarray(value, np.float32).astype(jnp.bfloat16).astype(np.float32))


def taps_at(diff, taps, sigma):
    total = jnp.zeros(diff.shape, F32)
    for k in range(-3 * sigma, 3 * sigma + 1):
        total = jnp.where(diff == k, F32(rounded(taps[k + HALO])), total)
    return total


def margin(channels):
    return 0 if channels <= WIDE else LANES


def in_hbm(x):
    return pltpu.with_memory_space_constraint(x, pltpu.MemorySpace.HBM)


def iota(shape, axis):
    return lax.broadcasted_iota(jnp.int32, shape, axis)


def tables_kernel(channels, taps_ref, main_ref, halo_ref, *rest):
    x_refs, far_refs, box_ref = rest[:SMAX], rest[SMAX : 2 * SMAX], rest[2 * SMAX]
    odd = odd_tile()
    taps = tap_table()
    for index in range(SMAX):
        sigma = index + 1
        rows = pl.ds(index * TILE_Y, TILE_Y)
        out_y, lane = iota((TILE_Y, LANES), 0), iota((TILE_Y, LANES), 1)
        main_ref[rows, :] = taps_at(lane - out_y, taps[index], sigma).astype(BF16)
        slot, part = lane // (2 * HALO), lane % (2 * HALO)
        in_y = jnp.where(part < HALO, part - HALO, part - HALO + TILE_Y)
        halo = taps_at(in_y - out_y, taps[index], sigma)
        for member in range(PACK):
            halo_ref[member, rows, :] = jnp.where(slot == member, halo, F32(0.0)).astype(BF16)
        reach = 3 * sigma
        for ref, shift in ((x_refs[index], choose(odd, -reach, 0)), (far_refs[index], choose(odd, TILE_X, -reach))):
            row, col = iota(ref.shape, 0), iota(ref.shape, 1)
            first = 0 if ref.shape[0] == PT * TILE_X else odd * HALF
            out_x = first + row // (PT * HALF) * HALF + row % HALF
            weight = taps_at(col // PT - out_x + shift, taps[index], sigma)
            ref[...] = jnp.where(row % (PT * HALF) // HALF == col % PT, weight, F32(0.0)).astype(BF16)
    for scale in range(NSC):
        width, dilation = taps_ref[0, scale], taps_ref[1, scale]
        shape = box_ref.shape[1:]
        diff = iota(shape, 0) - (shape[0] - shape[1]) // 2 - iota(shape, 1)
        hit = jnp.zeros(shape, F32)
        for step in range(WMAX):
            offset = jnp.where(step < width, dilation * (step - (width - 1) // 2), 2 * channels)
            hit = jnp.where(diff == offset, F32(1.0), hit)
        box_ref[scale] = hit.astype(BF16)


def tables(spectral_taps, channels):
    shapes = [(SMAX * TILE_Y, LANES), (PACK, SMAX * TILE_Y, LANES)]
    shapes += [(PT * TILE_X, (TILE_X + 3 * (i + 1)) * PT) for i in range(SMAX)]
    shapes += [(PT * (HALF if 3 * (i + 1) <= HALF else TILE_X), 3 * (i + 1) * PT) for i in range(SMAX)]
    wide = min(channels, WIDE)
    shapes += [(NSC, wide + 2 * margin(channels), wide)]
    return pl.pallas_call(
        functools.partial(tables_kernel, channels),
        out_shape=[jax.ShapeDtypeStruct(s, BF16) for s in shapes],
        in_specs=[pl.BlockSpec(memory_space=pltpu.SMEM)],
        out_specs=[pl.BlockSpec(memory_space=pltpu.VMEM)] * len(shapes),
        compiler_params=pltpu.CompilerParams(vmem_limit_bytes=16 * 2**20),
        cost_estimate=pl.CostEstimate(flops=10**7, bytes_accessed=4 * 10**6, transcendentals=0),
        name="tables",
    )(spectral_taps)


def pack_kernel(cube_ref, cover_hbm, out_ref, land_ref, cover_ref, turned_ref, sums_ref, sems):
    ch, ny, nx = cube_ref.shape
    n_rows, spans = ny // TILE_Y, nx // LANES
    n_cols, tiles = nx // TILE_X, LANES // TILE_X
    copies = [pltpu.make_async_copy(cube_ref.at[c], land_ref.at[c], sems.at[c]) for c in range(ch)]
    cover_copy = pltpu.make_async_copy(cover_hbm, cover_ref, sems.at[ch])
    cover_copy.start()
    for copy in copies:
        copy.start()
    sums_ref[...] = jnp.zeros(sums_ref.shape, F32)
    cover_copy.wait()
    tile_x, tile_y = cover_ref.shape
    eye = jnp.where(iota((tile_y, tile_y), 0) == iota((tile_y, tile_y), 1), F32(1.0), F32(0.0)).astype(BF16)
    cover = lax.dot_general(eye, cover_ref[...].astype(F32).astype(BF16), NT, preferred_element_type=F32).astype(BF16)

    def transpose(span, wait):
        at = span * LANES if isinstance(span, int) else pl.multiple_of(span * LANES, LANES)
        widen = jnp.where(iota((tile_x, LANES), 0) == span * tiles + iota((tile_x, LANES), 1) // PT, F32(1.0), F32(0.0))
        wide = jnp.dot(cover, widen.astype(BF16), preferred_element_type=F32)
        mask = jnp.broadcast_to(wide[:, None, :], (tile_y, PT, LANES)).reshape(ny, LANES) > 0.5
        for c in range(ch):
            if wait:
                copies[c].wait()
            plane = jnp.where(mask, land_ref[c, :, pl.ds(at, LANES)].astype(F32), F32(0.0))
            sums_ref[c : c + 1, :] += jnp.sum(plane * plane, axis=0, keepdims=True)
            turned = plane.T
            for r in range(n_rows):
                turned_ref[span, r, c * TURN : c * TURN + LANES, :] = turned[:, r * TILE_Y : (r + 1) * TILE_Y]

    def send(span, firsts):
        lane = iota((ch, LANES), 1)
        for t in range(tiles):
            for index, halo_group in enumerate(HALO_GROUPS):
                halos = [firsts[index]] * n_rows
                for x in range(index * PACK, min((index + 1) * PACK, TILE_X)):
                    slot, group = x % PACK * 2 * HALO, column_group(x)
                    columns = [turned_ref[span, r, pl.ds(t * TILE_X + x, ch, stride=TURN), :] for r in range(n_rows)]
                    ends = [jnp.zeros((ch, LANES), F32)]
                    around = ends + columns + ends
                    for r in range(n_rows):
                        dest = r * n_cols + span * tiles + t
                        out_ref[dest, group * ch : (group + 1) * ch, :] = columns[r].astype(BF16)
                        edge = pltpu.roll(jnp.where(lane < LANES // 2, around[r + 2], around[r]), slot + HALO, 1)
                        halos[r] = jnp.where((lane >= slot) & (lane < slot + 2 * HALO), edge, halos[r])
                for r in range(n_rows):
                    dest = r * n_cols + span * tiles + t
                    out_ref[dest, halo_group * ch : (halo_group + 1) * ch, :] = halos[r].astype(BF16)

    if spans == 1:
        transpose(0, True)
    else:
        for copy in copies:
            copy.wait()
        lax.fori_loop(0, spans, lambda span, carry: (transpose(span, False), carry)[1], 0)

    squares = jnp.minimum(jnp.sum(sums_ref[...], axis=1, keepdims=True) * F32(0.25), F32(BIG))
    high = squares.astype(BF16).astype(F32)
    mid = (squares - high).astype(BF16).astype(F32)
    low = squares - high - mid
    lane = iota((ch, LANES), 1)
    put = lambda at, value, base: jnp.where(lane == at, jnp.broadcast_to(value, (ch, LANES)), base)
    zeros = jnp.zeros((ch, LANES), F32)
    firsts = (put(LANES - 1, mid, put(LANES - 2, high, zeros)), put(LANES - 2, low, zeros), zeros)
    if spans == 1:
        send(0, firsts)
    else:
        lax.fori_loop(0, spans, lambda span, carry: (send(span, firsts), carry)[1], 0)


def pack(cube, footprint):
    ch, ny, nx = cube.shape
    n_rows, n_cols, spans = ny // TILE_Y, nx // TILE_X, nx // LANES
    need = 2 * ch * 4 * ny * nx
    return pl.pallas_call(
        pack_kernel,
        out_shape=jax.ShapeDtypeStruct((n_rows * n_cols, GROUPS * ch, LANES), BF16),
        in_specs=[pl.BlockSpec(memory_space=pltpu.MemorySpace.HBM)] * 2,
        out_specs=pl.BlockSpec(memory_space=pltpu.VMEM),
        scratch_shapes=[
            pltpu.VMEM((ch, ny, nx), BF16),
            pltpu.VMEM((nx // PT, ny // PT), jnp.int32),
            pltpu.VMEM((spans, n_rows, ch * TURN, TILE_Y), F32),
            pltpu.VMEM((ch, LANES), F32),
            pltpu.SemaphoreType.DMA((ch + 1,)),
        ],
        compiler_params=pltpu.CompilerParams(vmem_limit_bytes=need + 12 * 2**20),
        name="pack",
    )(in_hbm(cube), in_hbm(footprint.T))


def cut_kernel(far, own_ref, out_ref):
    odd = odd_tile()
    first = (odd if far else 1 - odd) * (GROUPS - SIDE)
    out_ref[...] = own_ref[:, pl.ds(first, SIDE)]


def cut(own, far):
    senders, _, ch, lanes = own.shape
    return pl.pallas_call(
        functools.partial(cut_kernel, far),
        out_shape=jax.ShapeDtypeStruct((senders, SIDE, ch, lanes), BF16),
        in_specs=[pl.BlockSpec(memory_space=pltpu.VMEM)],
        out_specs=pl.BlockSpec(memory_space=pltpu.VMEM),
        compiler_params=pltpu.CompilerParams(vmem_limit_bytes=6 * 2**20 if senders <= 32 else 24 * 2**20),
        name="cut_far" if far else "cut_near",
    )(own)


def load(ref, first, part, group):
    block = ref[pl.ds(first, part), group].astype(F32)
    return block.reshape(part * ref.shape[2], LANES).astype(BF16)


def y_pass(ref, first, part, group, halo_group, member, main_ref, halo_ref, rows_ref, x):
    data = jnp.concatenate([load(ref, first, part, group), load(ref, first, part, halo_group)], axis=1)
    band = jnp.concatenate([main_ref[...], halo_ref[member]], axis=1)
    rows = lax.dot_general(band, data, NT, preferred_element_type=F32).astype(BF16)
    rows_ref[:, :, x] = rows.reshape(SMAX, TILE_Y // PT, PT, rows.shape[1])


def x_pass(rows_ref, kind, group, start, count, weights_ref):
    slab = rows_ref[kind, group, pl.ds(start, count)]
    slab = slab.reshape(count * PT, slab.shape[-1])
    return jnp.dot(weights_ref[...], slab, preferred_element_type=F32)


def scale_rows(sigma_ref, taps_ref, cover_ref, footprint_ref, own_ref, first, part):
    lane = iota((8, 2 * LANES), 1)
    pick = jnp.where((lane >= LANES - 2) & (lane < LANES) | (lane == 2 * LANES - 2), F32(1.0), F32(0.0)).astype(BF16)
    both = jnp.concatenate([load(own_ref, first, part, group) for group in HALO_GROUPS[:2]], axis=1)
    squares = lax.dot_general(pick, both, NT, preferred_element_type=F32) * F32(4.0)
    count = jnp.maximum(jnp.sum(footprint_ref[...].astype(F32), keepdims=True) * F32(PT * PT), F32(1.0))
    noise = jnp.sqrt(squares / count + F32(1e-06))
    tile_x, tile_y = lax.axis_index("tx") * (TILE_X // PT), lax.axis_index("ty") * (TILE_Y // PT)
    seen = jnp.zeros(noise.shape, F32)
    for group in range(TILE_Y // PT):
        seen = jnp.where(iota(noise.shape, 0) == group, cover_ref[tile_x, tile_y + group].astype(F32), seen)
    energy = [F32(float(np.sum(t * t, dtype=np.float32))) for t in tap_table()]
    for scale in range(NSC):
        width = jnp.full(noise.shape, taps_ref[0, scale], jnp.int32).astype(F32)
        knorm = jnp.full(noise.shape, energy[0], F32)
        for index in range(1, SMAX):
            knorm = jnp.where(sigma_ref[scale] == index + 1, energy[index], knorm)
        yield scale, seen / (noise * (knorm / jnp.sqrt(width)) * width)


def begin_kernel(sigma_ref, taps_ref, cover_ref, footprint_ref, own_ref, near_ref, main_ref, halo_ref, *rest):
    x_refs, sum_ref, scale_ref, rows_ref = rest[:SMAX], *rest[SMAX : SMAX + 3]
    senders, _, ch, _ = own_ref.shape
    part = min(senders, WIDE // ch)
    odd = odd_tile()

    def one(index, carry):
        first = index * part
        passed = functools.partial(y_pass, main_ref=main_ref, halo_ref=halo_ref, rows_ref=rows_ref)
        for i in range(HALO):
            where = [choose(odd, a, b) for a, b in zip(left_column(i), right_column(i))]
            passed(near_ref, first, part, *where, x=choose(odd, i, TILE_X + i))
        for x in range(TILE_X):
            passed(own_ref, first, part, *right_column(x), x=choose(odd, HALO + x, x))
        lanes = pl.ds(pl.multiple_of(first * ch, part * ch), part * ch)
        for scale, value in scale_rows(sigma_ref, taps_ref, cover_ref, footprint_ref, own_ref, first, part):
            scale_ref[scale, :, lanes] = value
        for group in range(TILE_Y // PT):
            for kind in range(SMAX):
                reach = 3 * (kind + 1)
                start = choose(odd, HALO - reach, 0)
                field = x_pass(rows_ref, kind, group, start, TILE_X + reach, x_refs[kind])
                sum_ref[kind, group, :, :, lanes] = field.reshape(2, PT * HALF, part * ch)
        return carry

    if senders == part:
        one(0, 0)
    else:
        lax.fori_loop(0, senders // part, one, 0)


def begin(kernel_sigmas, spectral_taps, footprint, own, near, main, halo, weights):
    senders, _, ch, _ = own.shape
    channels = senders * ch
    wide = min(channels, WIDE)
    rows = (SMAX, TILE_Y // PT, TILE_X + HALO, PT, wide)
    sums = (SMAX, TILE_Y // PT, 2, PT * HALF, channels)
    smem = pl.BlockSpec(memory_space=pltpu.SMEM)
    vmem = pl.BlockSpec(memory_space=pltpu.VMEM)
    limit = 2 * int(np.prod(rows)) + 6 * 2**20 if channels <= WIDE else 62 * 2**20
    return pl.pallas_call(
        begin_kernel,
        out_shape=[jax.ShapeDtypeStruct(sums, F32), jax.ShapeDtypeStruct((NSC, TILE_Y // PT, channels), F32)],
        in_specs=[smem] * 3 + [vmem] * (5 + len(weights)),
        out_specs=[vmem] * 2,
        scratch_shapes=[pltpu.VMEM(rows, BF16)],
        compiler_params=pltpu.CompilerParams(vmem_limit_bytes=limit),
        cost_estimate=pl.CostEstimate(flops=10**9, bytes_accessed=8 * 10**6, transcendentals=0),
        name="begin",
    )(kernel_sigmas, spectral_taps, footprint.T, footprint.T, own, near, main, halo, *weights)


def finish_kernel(sigma_ref, far_ref, sum_ref, scale_ref, main_ref, halo_ref, *rest):
    far_refs, box_ref, out_ref, rows_ref, stage_ref, sems = rest[:SMAX], *rest[SMAX : SMAX + 5]
    smooth_refs = rest[SMAX + 5 :]
    senders, _, ch, _ = far_ref.shape
    channels = senders * ch
    part = min(senders, WIDE // ch)
    odd = odd_tile()
    slots, _, tall = stage_ref.shape[:3]
    span, phases = tall // PT, TILE_Y // tall
    wide, edge = min(channels, WIDE), margin(channels)

    def out_copy(phase, slot, scale):
        there = out_ref.at[scale, pl.ds(phase * tall, tall)]
        return pltpu.make_async_copy(stage_ref.at[slot, scale], there, sems.at[slot, scale])

    def far_y(first):
        for i in range(HALO):
            where = [choose(odd, a, b) for a, b in zip(right_column(i), left_column(i))]
            y_pass(far_ref, first, part, *where, main_ref, halo_ref, rows_ref, i)

    def far_x(first, phase):
        lanes = slice(first * ch, (first + part) * ch)
        for kind in range(SMAX):
            reach = 3 * (kind + 1)
            for row in range(span):
                group = phase * span + row
                added = x_pass(rows_ref, kind, group, choose(odd, 0, HALO - reach), reach, far_refs[kind])
                added = added.reshape(-1, PT * HALF, part * ch)
                if added.shape[0] == 2:
                    smooth_refs[phase][kind, row, :, :, lanes] = (sum_ref[kind, group, :, :, lanes] + added).astype(BF16)
                else:
                    smooth_refs[phase][kind, row, odd, :, lanes] = (sum_ref[kind, group, odd, :, lanes] + added[0]).astype(BF16)
                    smooth_refs[phase][kind, row, 1 - odd, :, lanes] = sum_ref[kind, group, 1 - odd, :, lanes].astype(BF16)

    def box_pass(phase, slot):
        for scale in range(NSC):
            if phase >= slots:
                out_copy(phase - slots, slot, scale).wait()
            for row in range(span):
                group = phase * span + row
                for at in range(0, channels, wide):
                    lanes, first = slice(at, at + wide), at - edge
                    low, high = max(first, 0), min(at + wide + edge, channels)
                    field = smooth_refs[phase][sigma_ref[scale] - 1, row, :, :, low:high]
                    field = field.reshape(PT * TILE_X, high - low)
                    boxed = jnp.dot(field, box_ref[scale, low - first : high - first], preferred_element_type=F32)
                    scaled = (boxed * scale_ref[scale, group : group + 1, lanes]).astype(BF16)
                    scaled = scaled.reshape(2, PT, HALF, wide)
                    for half in range(2):
                        stage_ref[slot, scale, row * PT : (row + 1) * PT, half * HALF : (half + 1) * HALF, lanes] = scaled[half]
            out_copy(phase, slot, scale).start()

    whole = senders == part
    for first in range(0, senders, part):
        far_y(first)
        if not whole:
            for phase in range(phases):
                far_x(first, phase)
    for phase in range(phases):
        if whole:
            far_x(0, phase)
        box_pass(phase, phase % slots)
    for phase in range(phases - slots, phases):
        for scale in range(NSC):
            out_copy(phase, phase % slots, scale).wait()


def finish(kernel_sigmas, far, sums, scales, main, halo, weights, box):
    senders, _, ch, _ = far.shape
    channels = senders * ch
    wide = min(channels, WIDE)
    span = SPAN if channels <= WIDE else 1
    phases = TILE_Y // PT // span
    slots = min(2, phases)
    rows = (SMAX, TILE_Y // PT, HALO, PT, wide)
    need = 2 * int(np.prod(rows)) + 2 * channels * (slots * span * NSC + SMAX * TILE_Y // PT) * PT * TILE_X
    vmem = pl.BlockSpec(memory_space=pltpu.VMEM)
    return pl.pallas_call(
        finish_kernel,
        out_shape=jax.ShapeDtypeStruct((NSC, TILE_Y, TILE_X, channels), BF16),
        in_specs=[pl.BlockSpec(memory_space=pltpu.SMEM)] + [vmem] * (6 + len(weights)),
        out_specs=pl.BlockSpec(memory_space=pltpu.MemorySpace.HBM),
        scratch_shapes=[
            pltpu.VMEM(rows, BF16),
            pltpu.VMEM((slots, NSC, span * PT, TILE_X, channels), BF16),
            pltpu.SemaphoreType.DMA((slots, NSC)),
        ]
        + [pltpu.VMEM((SMAX, span, 2, PT * HALF, channels), BF16)] * phases,
        compiler_params=pltpu.CompilerParams(
            vmem_limit_bytes=need + 6 * 2**20 if channels <= WIDE else 62 * 2**20
        ),
        name="finish",
    )(kernel_sigmas, far, sums, scales, main, halo, *weights, box)


def local(channel_cube, footprint, kernel_sigmas, spectral_taps):
    n_cols = lax.axis_size("tx")
    ch = channel_cube.shape[0]
    channels = ch * lax.axis_size("ty") * n_cols
    packed = pack(channel_cube, footprint)
    own = lax.all_to_all(packed, ("ty", "tx"), split_axis=0, concat_axis=0, tiled=True)
    own = own.reshape(own.shape[0], GROUPS, ch, LANES)
    far_pairs = [(i, i + 1) for i in range(1, n_cols - 1, 2)]
    near_pairs = [(i, i + 1) for i in range(0, n_cols - 1, 2)]
    both = lambda pairs: pairs + [(j, i) for i, j in pairs]
    far, near = cut(own, True), cut(own, False)
    far = lax.ppermute(far, "tx", both(far_pairs))
    near = lax.ppermute(near, "tx", both(near_pairs))
    main, halo, *weights, box = tables(spectral_taps, channels)
    sums, scales = begin(kernel_sigmas, spectral_taps, footprint, own, near, main, halo, weights[:SMAX])
    return finish(kernel_sigmas, far, sums, scales, main, halo, weights[SMAX:], box)


def solution(mesh):
    placed = (P(("ty", "tx"), None, None), P(), P(), P())
    return jax.shard_map(local, mesh=mesh, in_specs=placed, out_specs=P(None, "ty", "tx", None), check_vma=False)
```

```python
import functools

import jax
import jax.numpy as jnp
import numpy as np
from jax import lax
from jax.experimental import pallas as pl
from jax.experimental.pallas import tpu as pltpu
from jax.sharding import PartitionSpec as P


TILE_Y = 128
TILE_X = 16
HALF = TILE_X // 2
NSC = 4
WMAX = 5
PT = 16
HALO = 9
SMAX = 3
REACH = [3 * (i + 1) for i in range(SMAX)]
LANES = 128
TURN = LANES + 8
PACK = 7
HALO_GROUPS = (1, 10, 17)
GROUPS = TILE_X + 4
SIDE = 11
FAR = HALO - 1
WIDE = 256
BF16 = jnp.bfloat16
F32 = jnp.float32
BIG = 3.3895313892515355e38
NT = (((1,), (1,)), ((), ()))


def column_group(x):
    return x if x == 0 else x + 1 if x < HALO else x + 2 if x < TILE_X - 1 else x + 3


def column(x, base=0):
    return column_group(x) - base, HALO_GROUPS[x // PACK] - base, x % PACK


def odd_tile():
    return lax.rem(lax.axis_index("tx"), 2)


def choose(flag, one, other):
    return jnp.where(flag == 1, jnp.int32(one), jnp.int32(other))


def tap_table():
    offsets = np.arange(-HALO, HALO + 1).astype(np.float32)
    rows = []
    for sigma in range(1, SMAX + 1):
        spread = np.float32(sigma)
        weights = np.exp(-offsets * offsets / (np.float32(2.0) * spread * spread))
        weights = np.where(np.abs(offsets) <= 3.0 * spread, weights, np.float32(0.0)).astype(np.float32)
        rows.append(weights / np.sum(weights, dtype=np.float32))
    return rows


def rounded(value):
    return float(np.asarray(value, np.float32).astype(jnp.bfloat16).astype(np.float32))


def taps_at(diff, taps, sigma):
    total = jnp.zeros(diff.shape, F32)
    for k in range(-3 * sigma, 3 * sigma + 1):
        total = jnp.where(diff == k, F32(rounded(taps[k + HALO])), total)
    return total


def margin(channels):
    return 0 if channels <= WIDE else LANES


def in_hbm(x):
    return pltpu.with_memory_space_constraint(x, pltpu.MemorySpace.HBM)


def iota(shape, axis):
    return lax.broadcasted_iota(jnp.int32, shape, axis)


def tables_kernel(channels, taps_ref, main_ref, halo_ref, *rest):
    near_refs, here_refs, far_refs, box_ref = rest[:SMAX], rest[SMAX : 2 * SMAX], rest[2 * SMAX : 3 * SMAX], rest[3 * SMAX]
    odd = odd_tile()
    taps = tap_table()
    for index in range(SMAX):
        sigma = index + 1
        rows = pl.ds(index * TILE_Y, TILE_Y)
        out_y, lane = iota((TILE_Y, LANES), 0), iota((TILE_Y, LANES), 1)
        main_ref[rows, :] = taps_at(lane - out_y, taps[index], sigma).astype(BF16)
        slot, part = lane // (2 * HALO), lane % (2 * HALO)
        in_y = jnp.where(part < HALO, part - HALO, part - HALO + TILE_Y)
        halo = taps_at(in_y - out_y, taps[index], sigma)
        for member in range(PACK):
            halo_ref[member, rows, :] = jnp.where(slot == member, halo, F32(0.0)).astype(BF16)
        reach = 3 * sigma
        shifts = (-reach, choose(odd, -reach, -1), choose(odd, HALO, -reach))
        for ref, shift in zip((near_refs[index], here_refs[index], far_refs[index]), shifts):
            row, col = iota(ref.shape, 0), iota(ref.shape, 1)
            weight = taps_at(col // PT - row % HALF + shift, taps[index], sigma)
            ref[...] = jnp.where(row // HALF == col % PT, weight, F32(0.0)).astype(BF16)
    for scale in range(NSC):
        width, dilation = taps_ref[0, scale], taps_ref[1, scale]
        shape = box_ref.shape[1:]
        diff = iota(shape, 0) - (shape[0] - shape[1]) // 2 - iota(shape, 1)
        hit = jnp.zeros(shape, F32)
        for step in range(WMAX):
            offset = jnp.where(step < width, dilation * (step - (width - 1) // 2), 2 * channels)
            hit = jnp.where(diff == offset, F32(1.0), hit)
        box_ref[scale] = hit.astype(BF16)


def tables(spectral_taps, channels):
    shapes = [(SMAX * TILE_Y, LANES), (PACK, SMAX * TILE_Y, LANES)]
    for counts in ([HALF + 2 * r for r in REACH], [HALO + r for r in REACH], [r - 1 for r in REACH]):
        shapes += [(PT * HALF, count * PT) for count in counts]
    wide = min(channels, WIDE)
    shapes += [(NSC, wide + 2 * margin(channels), wide)]
    return pl.pallas_call(
        functools.partial(tables_kernel, channels),
        out_shape=[jax.ShapeDtypeStruct(s, BF16) for s in shapes],
        in_specs=[pl.BlockSpec(memory_space=pltpu.SMEM)],
        out_specs=[pl.BlockSpec(memory_space=pltpu.VMEM)] * len(shapes),
        compiler_params=pltpu.CompilerParams(vmem_limit_bytes=16 * 2**20),
        cost_estimate=pl.CostEstimate(flops=10**7, bytes_accessed=4 * 10**6, transcendentals=0),
        name="tables",
    )(spectral_taps)


def pack_kernel(cube_ref, cover_hbm, out_ref, land_ref, cover_ref, turned_ref, sums_ref, sems):
    ch, ny, nx = cube_ref.shape
    n_rows, spans = ny // TILE_Y, nx // LANES
    n_cols, tiles = nx // TILE_X, LANES // TILE_X
    copies = [pltpu.make_async_copy(cube_ref.at[c], land_ref.at[c], sems.at[c]) for c in range(ch)]
    cover_copy = pltpu.make_async_copy(cover_hbm, cover_ref, sems.at[ch])
    cover_copy.start()
    for copy in copies:
        copy.start()
    sums_ref[...] = jnp.zeros(sums_ref.shape, F32)
    cover_copy.wait()
    tile_x, tile_y = cover_ref.shape
    eye = jnp.where(iota((tile_y, tile_y), 0) == iota((tile_y, tile_y), 1), F32(1.0), F32(0.0)).astype(BF16)
    cover = lax.dot_general(eye, cover_ref[...].astype(F32).astype(BF16), NT, preferred_element_type=F32).astype(BF16)

    def transpose(span, wait):
        at = span * LANES if isinstance(span, int) else pl.multiple_of(span * LANES, LANES)
        widen = jnp.where(iota((tile_x, LANES), 0) == span * tiles + iota((tile_x, LANES), 1) // PT, F32(1.0), F32(0.0))
        wide = jnp.dot(cover, widen.astype(BF16), preferred_element_type=F32)
        mask = jnp.broadcast_to(wide[:, None, :], (tile_y, PT, LANES)).reshape(ny, LANES) > 0.5
        for c in range(ch):
            if wait:
                copies[c].wait()
            plane = jnp.where(mask, land_ref[c, :, pl.ds(at, LANES)].astype(F32), F32(0.0))
            sums_ref[c : c + 1, :] += jnp.sum(plane * plane, axis=0, keepdims=True)
            turned = plane.T
            for r in range(n_rows):
                turned_ref[span, r, c * TURN : c * TURN + LANES, :] = turned[:, r * TILE_Y : (r + 1) * TILE_Y]

    def place(span, t, columns, group, slot, halos):
        ends = [jnp.zeros((ch, LANES), F32)]
        around = ends + columns + ends
        lane = iota((ch, LANES), 1)
        for r in range(n_rows):
            out_ref[r * n_cols + span * tiles + t, group * ch : (group + 1) * ch, :] = columns[r].astype(BF16)
            edge = pltpu.roll(jnp.where(lane < LANES // 2, around[r + 2], around[r]), slot + HALO, 1)
            halos[r] = jnp.where((lane >= slot) & (lane < slot + 2 * HALO), edge, halos[r])

    def beyond(span, t, r):
        x = t * TILE_X + TILE_X if t % 2 else t * TILE_X - 1
        if 0 <= x < LANES:
            return turned_ref[span, r, pl.ds(x, ch, stride=TURN), :]
        if spans == 1:
            return jnp.zeros((ch, LANES), F32)
        there = span + 1 if x > 0 else span - 1
        inside = jnp.where((there >= 0) & (there < spans), F32(1.0), F32(0.0))
        there = jnp.minimum(jnp.maximum(there, 0), spans - 1)
        return turned_ref[there, r, pl.ds(x % LANES, ch, stride=TURN), :] * inside

    def send(span, firsts):
        for t in range(tiles):
            for index, halo_group in enumerate(HALO_GROUPS):
                halos = [firsts[index]] * n_rows
                for x in range(index * PACK, min((index + 1) * PACK, TILE_X)):
                    slot, group = x % PACK * 2 * HALO, column_group(x)
                    columns = [turned_ref[span, r, pl.ds(t * TILE_X + x, ch, stride=TURN), :] for r in range(n_rows)]
                    place(span, t, columns, group, slot, halos)
                if index == len(HALO_GROUPS) - 1:
                    place(span, t, [beyond(span, t, r) for r in range(n_rows)], GROUPS - 1, 2 * 2 * HALO, halos)
                for r in range(n_rows):
                    dest = r * n_cols + span * tiles + t
                    out_ref[dest, halo_group * ch : (halo_group + 1) * ch, :] = halos[r].astype(BF16)

    if spans == 1:
        transpose(0, True)
    else:
        for copy in copies:
            copy.wait()
        lax.fori_loop(0, spans, lambda span, carry: (transpose(span, False), carry)[1], 0)

    squares = jnp.minimum(jnp.sum(sums_ref[...], axis=1, keepdims=True) * F32(0.25), F32(BIG))
    high = squares.astype(BF16).astype(F32)
    mid = (squares - high).astype(BF16).astype(F32)
    low = squares - high - mid
    lane = iota((ch, LANES), 1)
    put = lambda at, value, base: jnp.where(lane == at, jnp.broadcast_to(value, (ch, LANES)), base)
    zeros = jnp.zeros((ch, LANES), F32)
    firsts = (put(LANES - 1, mid, put(LANES - 2, high, zeros)), put(LANES - 2, low, zeros), zeros)
    if spans == 1:
        send(0, firsts)
    else:
        lax.fori_loop(0, spans, lambda span, carry: (send(span, firsts), carry)[1], 0)


def pack(cube, footprint):
    ch, ny, nx = cube.shape
    n_rows, n_cols, spans = ny // TILE_Y, nx // TILE_X, nx // LANES
    need = 2 * ch * 4 * ny * nx
    return pl.pallas_call(
        pack_kernel,
        out_shape=jax.ShapeDtypeStruct((n_rows * n_cols, GROUPS * ch, LANES), BF16),
        in_specs=[pl.BlockSpec(memory_space=pltpu.MemorySpace.HBM)] * 2,
        out_specs=pl.BlockSpec(memory_space=pltpu.VMEM),
        scratch_shapes=[
            pltpu.VMEM((ch, ny, nx), BF16),
            pltpu.VMEM((nx // PT, ny // PT), jnp.int32),
            pltpu.VMEM((spans, n_rows, ch * TURN, TILE_Y), F32),
            pltpu.VMEM((ch, LANES), F32),
            pltpu.SemaphoreType.DMA((ch + 1,)),
        ],
        compiler_params=pltpu.CompilerParams(vmem_limit_bytes=need + 12 * 2**20),
        name="pack",
    )(in_hbm(cube), in_hbm(footprint.T))


def cut_kernel(far, own_ref, out_ref):
    odd = odd_tile()
    first = choose(odd, GROUPS - 1 - SIDE, 1) if far else choose(odd, 0, GROUPS - 1 - SIDE)
    out_ref[...] = own_ref[:, pl.ds(first, out_ref.shape[1])]


def cut(own, far):
    senders, _, ch, lanes = own.shape
    return pl.pallas_call(
        functools.partial(cut_kernel, far),
        out_shape=jax.ShapeDtypeStruct((senders, SIDE - 1 if far else SIDE, ch, lanes), BF16),
        in_specs=[pl.BlockSpec(memory_space=pltpu.VMEM)],
        out_specs=pl.BlockSpec(memory_space=pltpu.VMEM),
        compiler_params=pltpu.CompilerParams(vmem_limit_bytes=6 * 2**20 if senders <= 32 else 24 * 2**20),
        name="cut_far" if far else "cut_near",
    )(own)


def load(ref, first, part, group):
    block = ref[pl.ds(first, part), group].astype(F32)
    return block.reshape(part * ref.shape[2], LANES).astype(BF16)


def y_pass(ref, first, part, group, halo_group, member, main_ref, halo_ref, rows_ref, x):
    data = jnp.concatenate([load(ref, first, part, group), load(ref, first, part, halo_group)], axis=1)
    band = jnp.concatenate([main_ref[...], halo_ref[member]], axis=1)
    rows = lax.dot_general(band, data, NT, preferred_element_type=F32).astype(BF16)
    rows_ref[:, :, x] = rows.reshape(SMAX, TILE_Y // PT, PT, rows.shape[1])


def x_pass(rows_ref, kind, group, start, count, weights_ref):
    slab = rows_ref[kind, group, pl.ds(start, count)]
    slab = slab.reshape(count * PT, slab.shape[-1])
    return jnp.dot(weights_ref[...], slab, preferred_element_type=F32)


def scale_rows(sigma_ref, taps_ref, cover_ref, footprint_ref, own_ref, first, part):
    lane = iota((8, 2 * LANES), 1)
    pick = jnp.where((lane >= LANES - 2) & (lane < LANES) | (lane == 2 * LANES - 2), F32(1.0), F32(0.0)).astype(BF16)
    both = jnp.concatenate([load(own_ref, first, part, group) for group in HALO_GROUPS[:2]], axis=1)
    squares = lax.dot_general(pick, both, NT, preferred_element_type=F32) * F32(4.0)
    count = jnp.maximum(jnp.sum(footprint_ref[...].astype(F32), keepdims=True) * F32(PT * PT), F32(1.0))
    noise = jnp.sqrt(squares / count + F32(1e-06))
    tile_x, tile_y = lax.axis_index("tx") * (TILE_X // PT), lax.axis_index("ty") * (TILE_Y // PT)
    seen = jnp.zeros(noise.shape, F32)
    for group in range(TILE_Y // PT):
        seen = jnp.where(iota(noise.shape, 0) == group, cover_ref[tile_x, tile_y + group].astype(F32), seen)
    energy = [F32(float(np.sum(t * t, dtype=np.float32))) for t in tap_table()]
    for scale in range(NSC):
        width = jnp.full(noise.shape, taps_ref[0, scale], jnp.int32).astype(F32)
        knorm = jnp.full(noise.shape, energy[0], F32)
        for index in range(1, SMAX):
            knorm = jnp.where(sigma_ref[scale] == index + 1, energy[index], knorm)
        yield scale, seen / (noise * (knorm / jnp.sqrt(width)) * width)


def box_half(half, sigma_ref, scale_ref, box_ref, smooth_ref, stage_ref, out_ref, sems):
    channels = smooth_ref.shape[-1]
    wide, edge = min(channels, WIDE), margin(channels)
    copies = []
    for scale in range(NSC):
        for group in range(0, TILE_Y // PT, 2):
            for at in range(0, channels, wide):
                lanes, first = slice(at, at + wide), at - edge
                low, high = max(first, 0), min(at + wide + edge, channels)
                field = smooth_ref[sigma_ref[scale] - 1, group : group + 2, :, low:high].reshape(2 * PT * HALF, high - low)
                boxed = jnp.dot(field, box_ref[scale, low - first : high - first], preferred_element_type=F32)
                boxed = boxed.reshape(2, PT * HALF, wide)
                for row in range(2):
                    scaled = (boxed[row] * scale_ref[scale, group + row : group + row + 1, lanes]).astype(BF16)
                    rows = slice((group + row) * PT, (group + row + 1) * PT)
                    stage_ref[scale, rows, :, lanes] = scaled.reshape(PT, HALF, wide)
        there = out_ref.at[scale, :, pl.ds(pl.multiple_of(half * HALF, HALF), HALF)]
        copies.append(pltpu.make_async_copy(stage_ref.at[scale], there, sems.at[scale]))
        copies[-1].start()
    return copies


def begin_kernel(sigma_ref, taps_ref, cover_ref, footprint_ref, own_ref, near_ref, main_ref, halo_ref, *rest):
    near_refs, here_refs, box_ref = rest[:SMAX], rest[SMAX : 2 * SMAX], rest[2 * SMAX]
    out_ref, sum_ref, scale_ref, rows_ref, smooth_ref, stage_ref, sems = rest[2 * SMAX + 1 :]
    senders, _, ch, _ = own_ref.shape
    part = min(senders, WIDE // ch)
    groups = range(TILE_Y // PT)
    odd = odd_tile()

    def lanes_of(index):
        return pl.ds(pl.multiple_of(index * part * ch, part * ch), part * ch)

    def one(index, carry):
        first = index * part
        lanes = lanes_of(index)
        for scale, value in scale_rows(sigma_ref, taps_ref, cover_ref, footprint_ref, own_ref, first, part):
            scale_ref[scale, :, lanes] = value
        passed = functools.partial(y_pass, main_ref=main_ref, halo_ref=halo_ref, rows_ref=rows_ref)
        base = GROUPS - 1 - SIDE
        for i in range(HALO):
            where = [choose(odd, a, b) for a, b in zip(column(TILE_X - HALO + i, base), column(i))]
            passed(near_ref, first, part, *where, x=choose(odd, i, TILE_X + 1 + i))
        for x in range(TILE_X):
            passed(own_ref, first, part, *column(x), x=choose(odd, HALO + x, 1 + x))
        passed(own_ref, first, part, GROUPS - 1, HALO_GROUPS[-1], 2, x=choose(odd, HALO + TILE_X, 0))
        for group in groups:
            for kind, reach in enumerate(REACH):
                field = x_pass(rows_ref, kind, group, HALO - reach, HALF + 2 * reach, near_refs[kind])
                smooth_ref[kind, group, :, lanes] = field.astype(BF16)
        return carry

    def two(index, carry):
        lanes = lanes_of(index)
        for group in groups:
            for kind, reach in enumerate(REACH):
                start = choose(odd, HALO + HALF - reach, 0)
                sum_ref[kind, group, :, lanes] = x_pass(rows_ref, kind, group, start, HALO + reach, here_refs[kind])
        return carry

    if senders == part:
        one(0, 0)
    else:
        lax.fori_loop(0, senders // part, lambda index, carry: two(index, one(index, carry)), 0)
    copies = box_half(1 - odd, sigma_ref, scale_ref, box_ref, smooth_ref, stage_ref, out_ref, sems)
    if senders == part:
        two(0, 0)
    for copy in copies:
        copy.wait()


def begin(kernel_sigmas, spectral_taps, footprint, own, near, main, halo, weights, box):
    senders, _, ch, _ = own.shape
    channels = senders * ch
    wide = min(channels, WIDE)
    rows = (SMAX, TILE_Y // PT, TILE_X + HALO + 1, PT, wide)
    sums = (SMAX, TILE_Y // PT, PT * HALF, channels)
    stage = (NSC, TILE_Y, HALF, channels)
    smem = pl.BlockSpec(memory_space=pltpu.SMEM)
    vmem = pl.BlockSpec(memory_space=pltpu.VMEM)
    limit = 2 * int(np.prod(rows) + np.prod(sums) + np.prod(stage)) + 6 * 2**20 if channels <= WIDE else 62 * 2**20
    return pl.pallas_call(
        begin_kernel,
        out_shape=[
            jax.ShapeDtypeStruct((NSC, TILE_Y, TILE_X, channels), BF16),
            jax.ShapeDtypeStruct(sums, F32),
            jax.ShapeDtypeStruct((NSC, TILE_Y // PT, channels), F32),
        ],
        in_specs=[smem] * 3 + [vmem] * (6 + len(weights)),
        out_specs=[pl.BlockSpec(memory_space=pltpu.MemorySpace.HBM)] + [vmem] * 2,
        scratch_shapes=[
            pltpu.VMEM(rows, BF16),
            pltpu.VMEM(sums, BF16),
            pltpu.VMEM(stage, BF16),
            pltpu.SemaphoreType.DMA((NSC,)),
        ],
        compiler_params=pltpu.CompilerParams(vmem_limit_bytes=limit),
        cost_estimate=pl.CostEstimate(flops=10**9, bytes_accessed=8 * 10**6, transcendentals=0),
        name="begin",
    )(kernel_sigmas, spectral_taps, footprint.T, footprint.T, own, near, main, halo, *weights, box)


def finish_kernel(sigma_ref, _, far_ref, sum_ref, scale_ref, main_ref, halo_ref, *rest):
    far_refs, box_ref, out_ref, rows_ref, smooth_ref, stage_ref, sems = rest[:SMAX], *rest[SMAX:]
    senders, _, ch, _ = far_ref.shape
    part = min(senders, WIDE // ch)
    odd = odd_tile()
    for first in range(0, senders, part):
        lanes = slice(first * ch, (first + part) * ch)
        for i in range(FAR):
            pair = zip(column(1 + i, 1), column(TILE_X - HALO + i, GROUPS - 1 - SIDE))
            where = [choose(odd, a, b) for a, b in pair]
            y_pass(far_ref, first, part, *where, main_ref, halo_ref, rows_ref, i)
        for group in range(TILE_Y // PT):
            for kind, reach in enumerate(REACH):
                added = x_pass(rows_ref, kind, group, choose(odd, 0, HALO - reach), reach - 1, far_refs[kind])
                smooth_ref[kind, group, :, lanes] = (sum_ref[kind, group, :, lanes] + added).astype(BF16)
    for copy in box_half(odd, sigma_ref, scale_ref, box_ref, smooth_ref, stage_ref, out_ref, sems):
        copy.wait()


def finish(kernel_sigmas, out, far, sums, scales, main, halo, weights, box):
    senders, _, ch, _ = far.shape
    channels = senders * ch
    rows = (SMAX, TILE_Y // PT, FAR, PT, min(channels, WIDE))
    stage = (NSC, TILE_Y, HALF, channels)
    vmem = pl.BlockSpec(memory_space=pltpu.VMEM)
    hbm = pl.BlockSpec(memory_space=pltpu.MemorySpace.HBM)
    need = 2 * int(np.prod(rows) + np.prod(sums.shape) + np.prod(stage))
    return pl.pallas_call(
        finish_kernel,
        out_shape=jax.ShapeDtypeStruct(out.shape, BF16),
        in_specs=[pl.BlockSpec(memory_space=pltpu.SMEM), hbm] + [vmem] * (6 + len(weights)),
        out_specs=hbm,
        input_output_aliases={1: 0},
        scratch_shapes=[
            pltpu.VMEM(rows, BF16),
            pltpu.VMEM(sums.shape, BF16),
            pltpu.VMEM(stage, BF16),
            pltpu.SemaphoreType.DMA((NSC,)),
        ],
        compiler_params=pltpu.CompilerParams(
            vmem_limit_bytes=need + 6 * 2**20 if channels <= WIDE else 62 * 2**20
        ),
        name="finish",
    )(kernel_sigmas, out, far, sums, scales, main, halo, *weights, box)


def local(channel_cube, footprint, kernel_sigmas, spectral_taps):
    n_cols = lax.axis_size("tx")
    ch = channel_cube.shape[0]
    channels = ch * lax.axis_size("ty") * n_cols
    packed = pack(channel_cube, footprint)
    own = lax.all_to_all(packed, ("ty", "tx"), split_axis=0, concat_axis=0, tiled=True)
    own = own.reshape(own.shape[0], GROUPS, ch, LANES)
    far_pairs = [(i, i + 1) for i in range(1, n_cols - 1, 2)]
    near_pairs = [(i, i + 1) for i in range(0, n_cols - 1, 2)]
    both = lambda pairs: pairs + [(j, i) for i, j in pairs]
    far, near = cut(own, True), cut(own, False)
    far = lax.ppermute(far, "tx", both(far_pairs))
    near = lax.ppermute(near, "tx", both(near_pairs))
    main, halo, *weights, box = tables(spectral_taps, channels)
    out, sums, scales = begin(
        kernel_sigmas, spectral_taps, footprint, own, near, main, halo, weights[: 2 * SMAX], box
    )
    return finish(kernel_sigmas, out, far, sums, scales, main, halo, weights[2 * SMAX :], box)


def solution(mesh):
    placed = (P(("ty", "tx"), None, None), P(), P(), P())
    return jax.shard_map(local, mesh=mesh, in_specs=placed, out_specs=P(None, "ty", "tx", None), check_vma=False)
```

```python
import functools

import jax
import jax.numpy as jnp
import numpy as np
from jax import lax
from jax.experimental import pallas as pl
from jax.experimental.pallas import tpu as pltpu
from jax.sharding import PartitionSpec as P


TILE_Y = 128
TILE_X = 16
HALF = TILE_X // 2
NSC = 4
WMAX = 5
PT = 16
HALO = 9
SMAX = 3
REACH = [3 * (i + 1) for i in range(SMAX)]
LANES = 128
TURN = LANES + 8
PACK = 7
HALO_GROUPS = (1, 10, 17)
GROUPS = TILE_X + 4
SIDE = 11
RUN = 4
FAR = HALO - 1
WIDE = 256
BF16 = jnp.bfloat16
F32 = jnp.float32
BIG = 3.3895313892515355e38
NT = (((1,), (1,)), ((), ()))


def column_group(x):
    return x if x == 0 else x + 1 if x < HALO else x + 2 if x < TILE_X - 1 else x + 3


def column(x, base=0):
    return column_group(x) - base, HALO_GROUPS[x // PACK] - base, x % PACK


def odd_tile():
    return lax.rem(lax.axis_index("tx"), 2)


def choose(flag, one, other):
    return jnp.where(flag == 1, jnp.int32(one), jnp.int32(other))


def tap_table():
    offsets = np.arange(-HALO, HALO + 1).astype(np.float32)
    rows = []
    for sigma in range(1, SMAX + 1):
        spread = np.float32(sigma)
        weights = np.exp(-offsets * offsets / (np.float32(2.0) * spread * spread))
        weights = np.where(np.abs(offsets) <= 3.0 * spread, weights, np.float32(0.0)).astype(np.float32)
        rows.append(weights / np.sum(weights, dtype=np.float32))
    return rows


def rounded(value):
    return float(np.asarray(value, np.float32).astype(jnp.bfloat16).astype(np.float32))


def taps_at(diff, taps, sigma):
    total = jnp.zeros(diff.shape, F32)
    for k in range(-3 * sigma, 3 * sigma + 1):
        total = jnp.where(diff == k, F32(rounded(taps[k + HALO])), total)
    return total


def margin(channels):
    return 0 if channels <= WIDE else LANES


def in_hbm(x):
    return pltpu.with_memory_space_constraint(x, pltpu.MemorySpace.HBM)


def iota(shape, axis):
    return lax.broadcasted_iota(jnp.int32, shape, axis)


def tables_kernel(channels, taps_ref, main_ref, halo_ref, *rest):
    near_refs, here_refs, far_refs, box_ref = rest[:SMAX], rest[SMAX : 2 * SMAX], rest[2 * SMAX : 3 * SMAX], rest[3 * SMAX]
    odd = odd_tile()
    taps = tap_table()
    for index in range(SMAX):
        sigma = index + 1
        rows = pl.ds(index * TILE_Y, TILE_Y)
        out_y, lane = iota((TILE_Y, LANES), 0), iota((TILE_Y, LANES), 1)
        main_ref[rows, :] = taps_at(lane - out_y, taps[index], sigma).astype(BF16)
        slot, part = lane // (2 * HALO), lane % (2 * HALO)
        in_y = jnp.where(part < HALO, part - HALO, part - HALO + TILE_Y)
        halo = taps_at(in_y - out_y, taps[index], sigma)
        for member in range(PACK):
            halo_ref[member, rows, :] = jnp.where(slot == member, halo, F32(0.0)).astype(BF16)
        reach = 3 * sigma
        shifts = (-reach, choose(odd, -reach, -1), choose(odd, HALO, -reach))
        for ref, shift in zip((near_refs[index], here_refs[index], far_refs[index]), shifts):
            row, col = iota(ref.shape, 0), iota(ref.shape, 1)
            weight = taps_at(col // PT - row % HALF + shift, taps[index], sigma)
            ref[...] = jnp.where(row // HALF == col % PT, weight, F32(0.0)).astype(BF16)
    for scale in range(NSC):
        width, dilation = taps_ref[0, scale], taps_ref[1, scale]
        shape = box_ref.shape[1:]
        diff = iota(shape, 0) - (shape[0] - shape[1]) // 2 - iota(shape, 1)
        hit = jnp.zeros(shape, F32)
        for step in range(WMAX):
            offset = jnp.where(step < width, dilation * (step - (width - 1) // 2), 2 * channels)
            hit = jnp.where(diff == offset, F32(1.0), hit)
        box_ref[scale] = hit.astype(BF16)


def tables(spectral_taps, channels):
    shapes = [(SMAX * TILE_Y, LANES), (PACK, SMAX * TILE_Y, LANES)]
    for counts in ([HALF + 2 * r for r in REACH], [HALO + r for r in REACH], [r - 1 for r in REACH]):
        shapes += [(PT * HALF, count * PT) for count in counts]
    wide = min(channels, WIDE)
    shapes += [(NSC, wide + 2 * margin(channels), wide)]
    return pl.pallas_call(
        functools.partial(tables_kernel, channels),
        out_shape=[jax.ShapeDtypeStruct(s, BF16) for s in shapes],
        in_specs=[pl.BlockSpec(memory_space=pltpu.SMEM)],
        out_specs=[pl.BlockSpec(memory_space=pltpu.VMEM)] * len(shapes),
        compiler_params=pltpu.CompilerParams(vmem_limit_bytes=16 * 2**20),
        cost_estimate=pl.CostEstimate(flops=10**7, bytes_accessed=4 * 10**6, transcendentals=0),
        name="tables",
    )(spectral_taps)


def pack_kernel(cube_ref, cover_hbm, out_ref, land_ref, cover_ref, turned_ref, sums_ref, sems):
    ch, ny, nx = cube_ref.shape
    n_rows, spans = ny // TILE_Y, nx // LANES
    n_cols, tiles = nx // TILE_X, LANES // TILE_X
    copies = [pltpu.make_async_copy(cube_ref.at[c], land_ref.at[c], sems.at[c]) for c in range(ch)]
    cover_copy = pltpu.make_async_copy(cover_hbm, cover_ref, sems.at[ch])
    cover_copy.start()
    for copy in copies:
        copy.start()
    sums_ref[...] = jnp.zeros(sums_ref.shape, F32)
    cover_copy.wait()
    tile_x, tile_y = cover_ref.shape
    eye = jnp.where(iota((tile_y, tile_y), 0) == iota((tile_y, tile_y), 1), F32(1.0), F32(0.0)).astype(BF16)
    cover = lax.dot_general(eye, cover_ref[...].astype(F32).astype(BF16), NT, preferred_element_type=F32).astype(BF16)

    def transpose(span, wait):
        at = span * LANES if isinstance(span, int) else pl.multiple_of(span * LANES, LANES)
        widen = jnp.where(iota((tile_x, LANES), 0) == span * tiles + iota((tile_x, LANES), 1) // PT, F32(1.0), F32(0.0))
        wide = jnp.dot(cover, widen.astype(BF16), preferred_element_type=F32)
        mask = jnp.broadcast_to(wide[:, None, :], (tile_y, PT, LANES)).reshape(ny, LANES) > 0.5
        for c in range(ch):
            if wait:
                copies[c].wait()
            plane = jnp.where(mask, land_ref[c, :, pl.ds(at, LANES)].astype(F32), F32(0.0))
            sums_ref[c : c + 1, :] += jnp.sum(plane * plane, axis=0, keepdims=True)
            turned = plane.T
            for r in range(n_rows):
                turned_ref[span, r, c * TURN : c * TURN + LANES, :] = turned[:, r * TILE_Y : (r + 1) * TILE_Y]

    def place(span, t, columns, group, slot, halos):
        ends = [jnp.zeros((ch, LANES), F32)]
        around = ends + columns + ends
        lane = iota((ch, LANES), 1)
        for r in range(n_rows):
            out_ref[r * n_cols + span * tiles + t, group * ch : (group + 1) * ch, :] = columns[r].astype(BF16)
            edge = pltpu.roll(jnp.where(lane < LANES // 2, around[r + 2], around[r]), slot + HALO, 1)
            halos[r] = jnp.where((lane >= slot) & (lane < slot + 2 * HALO), edge, halos[r])

    def beyond(span, t, r):
        x = t * TILE_X + TILE_X if t % 2 else t * TILE_X - 1
        if 0 <= x < LANES:
            return turned_ref[span, r, pl.ds(x, ch, stride=TURN), :]
        if spans == 1:
            return jnp.zeros((ch, LANES), F32)
        there = span + 1 if x > 0 else span - 1
        inside = jnp.where((there >= 0) & (there < spans), F32(1.0), F32(0.0))
        there = jnp.minimum(jnp.maximum(there, 0), spans - 1)
        return turned_ref[there, r, pl.ds(x % LANES, ch, stride=TURN), :] * inside

    def send(span, firsts):
        for t in range(tiles):
            for index, halo_group in enumerate(HALO_GROUPS):
                halos = [firsts[index]] * n_rows
                for x in range(index * PACK, min((index + 1) * PACK, TILE_X)):
                    slot, group = x % PACK * 2 * HALO, column_group(x)
                    columns = [turned_ref[span, r, pl.ds(t * TILE_X + x, ch, stride=TURN), :] for r in range(n_rows)]
                    place(span, t, columns, group, slot, halos)
                if index == len(HALO_GROUPS) - 1:
                    place(span, t, [beyond(span, t, r) for r in range(n_rows)], GROUPS - 1, 2 * 2 * HALO, halos)
                for r in range(n_rows):
                    dest = r * n_cols + span * tiles + t
                    out_ref[dest, halo_group * ch : (halo_group + 1) * ch, :] = halos[r].astype(BF16)

    if spans == 1:
        transpose(0, True)
    else:
        for copy in copies:
            copy.wait()
        lax.fori_loop(0, spans, lambda span, carry: (transpose(span, False), carry)[1], 0)

    squares = jnp.minimum(jnp.sum(sums_ref[...], axis=1, keepdims=True) * F32(0.25), F32(BIG))
    high = squares.astype(BF16).astype(F32)
    mid = (squares - high).astype(BF16).astype(F32)
    low = squares - high - mid
    lane = iota((ch, LANES), 1)
    put = lambda at, value, base: jnp.where(lane == at, jnp.broadcast_to(value, (ch, LANES)), base)
    zeros = jnp.zeros((ch, LANES), F32)
    firsts = (put(LANES - 1, mid, put(LANES - 2, high, zeros)), put(LANES - 2, low, zeros), zeros)
    if spans == 1:
        send(0, firsts)
    else:
        lax.fori_loop(0, spans, lambda span, carry: (send(span, firsts), carry)[1], 0)


def pack(cube, footprint):
    ch, ny, nx = cube.shape
    n_rows, n_cols, spans = ny // TILE_Y, nx // TILE_X, nx // LANES
    need = 2 * ch * 4 * ny * nx
    return pl.pallas_call(
        pack_kernel,
        out_shape=jax.ShapeDtypeStruct((n_rows * n_cols, GROUPS * ch, LANES), BF16),
        in_specs=[pl.BlockSpec(memory_space=pltpu.MemorySpace.HBM)] * 2,
        out_specs=pl.BlockSpec(memory_space=pltpu.VMEM),
        scratch_shapes=[
            pltpu.VMEM((ch, ny, nx), BF16),
            pltpu.VMEM((nx // PT, ny // PT), jnp.int32),
            pltpu.VMEM((spans, n_rows, ch * TURN, TILE_Y), F32),
            pltpu.VMEM((ch, LANES), F32),
            pltpu.SemaphoreType.DMA((ch + 1,)),
        ],
        compiler_params=pltpu.CompilerParams(vmem_limit_bytes=need + 12 * 2**20),
        name="pack",
    )(in_hbm(cube), in_hbm(footprint.T))


def cut_kernel(far, own_ref, out_ref):
    odd = odd_tile()
    first = choose(odd, GROUPS - 1 - SIDE, 1) if far else choose(odd, 0, GROUPS - 1 - SIDE)
    out_ref[...] = own_ref[:, pl.ds(first, out_ref.shape[1])]


def cut(own, far):
    senders, _, ch, lanes = own.shape
    return pl.pallas_call(
        functools.partial(cut_kernel, far),
        out_shape=jax.ShapeDtypeStruct((senders, SIDE - 1 if far else SIDE, ch, lanes), BF16),
        in_specs=[pl.BlockSpec(memory_space=pltpu.VMEM)],
        out_specs=pl.BlockSpec(memory_space=pltpu.VMEM),
        compiler_params=pltpu.CompilerParams(vmem_limit_bytes=6 * 2**20 if senders <= 32 else 24 * 2**20),
        name="cut_far" if far else "cut_near",
    )(own)


def load(ref, first, part, group):
    block = ref[pl.ds(first, part), group].astype(F32)
    return block.reshape(part * ref.shape[2], LANES).astype(BF16)


def y_pass(ref, first, part, group, halo_group, member, main_ref, halo_ref, rows_ref, x):
    data = jnp.concatenate([load(ref, first, part, group), load(ref, first, part, halo_group)], axis=1)
    band = jnp.concatenate([main_ref[...], halo_ref[member]], axis=1)
    rows = lax.dot_general(band, data, NT, preferred_element_type=F32).astype(BF16)
    rows_ref[:, :, x] = rows.reshape(SMAX, TILE_Y // PT, PT, rows.shape[1])


def x_pass(rows_ref, kind, group, start, count, weights_ref):
    slab = rows_ref[kind, group, pl.ds(start, count)]
    slab = slab.reshape(count * PT, slab.shape[-1])
    return jnp.dot(weights_ref[...], slab, preferred_element_type=F32)


def scale_rows(sigma_ref, taps_ref, cover_ref, footprint_ref, own_ref, first, part):
    lane = iota((8, 2 * LANES), 1)
    pick = jnp.where((lane >= LANES - 2) & (lane < LANES) | (lane == 2 * LANES - 2), F32(1.0), F32(0.0)).astype(BF16)
    both = jnp.concatenate([load(own_ref, first, part, group) for group in HALO_GROUPS[:2]], axis=1)
    squares = lax.dot_general(pick, both, NT, preferred_element_type=F32) * F32(4.0)
    count = jnp.maximum(jnp.sum(footprint_ref[...].astype(F32), keepdims=True) * F32(PT * PT), F32(1.0))
    noise = jnp.sqrt(squares / count + F32(1e-06))
    tile_x, tile_y = lax.axis_index("tx") * (TILE_X // PT), lax.axis_index("ty") * (TILE_Y // PT)
    seen = jnp.zeros(noise.shape, F32)
    for group in range(TILE_Y // PT):
        seen = jnp.where(iota(noise.shape, 0) == group, cover_ref[tile_x, tile_y + group].astype(F32), seen)
    energy = [F32(float(np.sum(t * t, dtype=np.float32))) for t in tap_table()]
    for scale in range(NSC):
        width = jnp.full(noise.shape, taps_ref[0, scale], jnp.int32).astype(F32)
        knorm = jnp.full(noise.shape, energy[0], F32)
        for index in range(1, SMAX):
            knorm = jnp.where(sigma_ref[scale] == index + 1, energy[index], knorm)
        yield scale, seen / (noise * (knorm / jnp.sqrt(width)) * width)


def box_half(half, sigma_ref, scale_ref, box_ref, smooth_ref, stage_ref, out_ref, sems):
    channels = smooth_ref.shape[-1]
    wide, edge = min(channels, WIDE), margin(channels)
    copies = []
    for scale in range(NSC):
        for group in range(0, TILE_Y // PT, RUN):
            for at in range(0, channels, wide):
                lanes, first = slice(at, at + wide), at - edge
                low, high = max(first, 0), min(at + wide + edge, channels)
                field = smooth_ref[sigma_ref[scale] - 1, group : group + RUN, :, low:high].reshape(RUN * PT * HALF, high - low)
                boxed = jnp.dot(field, box_ref[scale, low - first : high - first], preferred_element_type=F32)
                boxed = boxed.reshape(RUN, PT * HALF, wide)
                for row in range(RUN):
                    scaled = (boxed[row] * scale_ref[scale, group + row : group + row + 1, lanes]).astype(BF16)
                    rows = slice((group + row) * PT, (group + row + 1) * PT)
                    stage_ref[scale, rows, :, lanes] = scaled.reshape(PT, HALF, wide)
        there = out_ref.at[scale, :, pl.ds(pl.multiple_of(half * HALF, HALF), HALF)]
        copies.append(pltpu.make_async_copy(stage_ref.at[scale], there, sems.at[scale]))
        copies[-1].start()
    return copies


def begin_kernel(sigma_ref, taps_ref, cover_ref, footprint_ref, own_ref, near_ref, main_ref, halo_ref, *rest):
    near_refs, here_refs, box_ref = rest[:SMAX], rest[SMAX : 2 * SMAX], rest[2 * SMAX]
    out_ref, sum_ref, scale_ref, rows_ref, smooth_ref, stage_ref, sems = rest[2 * SMAX + 1 :]
    senders, _, ch, _ = own_ref.shape
    part = min(senders, WIDE // ch)
    groups = range(TILE_Y // PT)
    odd = odd_tile()

    def lanes_of(index):
        return pl.ds(pl.multiple_of(index * part * ch, part * ch), part * ch)

    def one(index, carry):
        first = index * part
        lanes = lanes_of(index)
        for scale, value in scale_rows(sigma_ref, taps_ref, cover_ref, footprint_ref, own_ref, first, part):
            scale_ref[scale, :, lanes] = value
        passed = functools.partial(y_pass, main_ref=main_ref, halo_ref=halo_ref, rows_ref=rows_ref)
        base = GROUPS - 1 - SIDE
        for i in range(HALO):
            where = [choose(odd, a, b) for a, b in zip(column(TILE_X - HALO + i, base), column(i))]
            passed(near_ref, first, part, *where, x=choose(odd, i, TILE_X + 1 + i))
        for x in range(TILE_X):
            passed(own_ref, first, part, *column(x), x=choose(odd, HALO + x, 1 + x))
        passed(own_ref, first, part, GROUPS - 1, HALO_GROUPS[-1], 2, x=choose(odd, HALO + TILE_X, 0))
        for group in groups:
            for kind, reach in enumerate(REACH):
                field = x_pass(rows_ref, kind, group, HALO - reach, HALF + 2 * reach, near_refs[kind])
                smooth_ref[kind, group, :, lanes] = field.astype(BF16)
        return carry

    def two(index, carry):
        lanes = lanes_of(index)
        for group in groups:
            for kind, reach in enumerate(REACH):
                start = choose(odd, HALO + HALF - reach, 0)
                sum_ref[kind, group, :, lanes] = x_pass(rows_ref, kind, group, start, HALO + reach, here_refs[kind])
        return carry

    if senders == part:
        one(0, 0)
    else:
        lax.fori_loop(0, senders // part, lambda index, carry: two(index, one(index, carry)), 0)
    copies = box_half(1 - odd, sigma_ref, scale_ref, box_ref, smooth_ref, stage_ref, out_ref, sems)
    if senders == part:
        two(0, 0)
    for copy in copies:
        copy.wait()


def begin(kernel_sigmas, spectral_taps, footprint, own, near, main, halo, weights, box):
    senders, _, ch, _ = own.shape
    channels = senders * ch
    wide = min(channels, WIDE)
    rows = (SMAX, TILE_Y // PT, TILE_X + HALO + 1, PT, wide)
    sums = (SMAX, TILE_Y // PT, PT * HALF, channels)
    stage = (NSC, TILE_Y, HALF, channels)
    smem = pl.BlockSpec(memory_space=pltpu.SMEM)
    vmem = pl.BlockSpec(memory_space=pltpu.VMEM)
    limit = 2 * int(np.prod(rows) + np.prod(sums) + np.prod(stage)) + 6 * 2**20 if channels <= WIDE else 62 * 2**20
    return pl.pallas_call(
        begin_kernel,
        out_shape=[
            jax.ShapeDtypeStruct((NSC, TILE_Y, TILE_X, channels), BF16),
            jax.ShapeDtypeStruct(sums, F32),
            jax.ShapeDtypeStruct((NSC, TILE_Y // PT, channels), F32),
        ],
        in_specs=[smem] * 3 + [vmem] * (6 + len(weights)),
        out_specs=[pl.BlockSpec(memory_space=pltpu.MemorySpace.HBM)] + [vmem] * 2,
        scratch_shapes=[
            pltpu.VMEM(rows, BF16),
            pltpu.VMEM(sums, BF16),
            pltpu.VMEM(stage, BF16),
            pltpu.SemaphoreType.DMA((NSC,)),
        ],
        compiler_params=pltpu.CompilerParams(vmem_limit_bytes=limit),
        cost_estimate=pl.CostEstimate(flops=10**9, bytes_accessed=8 * 10**6, transcendentals=0),
        name="begin",
    )(kernel_sigmas, spectral_taps, footprint.T, footprint.T, own, near, main, halo, *weights, box)


def finish_kernel(sigma_ref, _, far_ref, sum_ref, scale_ref, main_ref, halo_ref, *rest):
    far_refs, box_ref, out_ref, rows_ref, smooth_ref, stage_ref, sems = rest[:SMAX], *rest[SMAX:]
    senders, _, ch, _ = far_ref.shape
    part = min(senders, WIDE // ch)
    odd = odd_tile()
    for first in range(0, senders, part):
        lanes = slice(first * ch, (first + part) * ch)
        for i in range(FAR):
            pair = zip(column(1 + i, 1), column(TILE_X - HALO + i, GROUPS - 1 - SIDE))
            where = [choose(odd, a, b) for a, b in pair]
            y_pass(far_ref, first, part, *where, main_ref, halo_ref, rows_ref, i)
        for group in range(TILE_Y // PT):
            for kind, reach in enumerate(REACH):
                added = x_pass(rows_ref, kind, group, choose(odd, 0, HALO - reach), reach - 1, far_refs[kind])
                smooth_ref[kind, group, :, lanes] = (sum_ref[kind, group, :, lanes] + added).astype(BF16)
    for copy in box_half(odd, sigma_ref, scale_ref, box_ref, smooth_ref, stage_ref, out_ref, sems):
        copy.wait()


def finish(kernel_sigmas, out, far, sums, scales, main, halo, weights, box):
    senders, _, ch, _ = far.shape
    channels = senders * ch
    rows = (SMAX, TILE_Y // PT, FAR, PT, min(channels, WIDE))
    stage = (NSC, TILE_Y, HALF, channels)
    vmem = pl.BlockSpec(memory_space=pltpu.VMEM)
    hbm = pl.BlockSpec(memory_space=pltpu.MemorySpace.HBM)
    need = 2 * int(np.prod(rows) + np.prod(sums.shape) + np.prod(stage))
    return pl.pallas_call(
        finish_kernel,
        out_shape=jax.ShapeDtypeStruct(out.shape, BF16),
        in_specs=[pl.BlockSpec(memory_space=pltpu.SMEM), hbm] + [vmem] * (6 + len(weights)),
        out_specs=hbm,
        input_output_aliases={1: 0},
        scratch_shapes=[
            pltpu.VMEM(rows, BF16),
            pltpu.VMEM(sums.shape, BF16),
            pltpu.VMEM(stage, BF16),
            pltpu.SemaphoreType.DMA((NSC,)),
        ],
        compiler_params=pltpu.CompilerParams(
            vmem_limit_bytes=need + 6 * 2**20 if channels <= WIDE else 62 * 2**20
        ),
        name="finish",
    )(kernel_sigmas, out, far, sums, scales, main, halo, *weights, box)


def local(channel_cube, footprint, kernel_sigmas, spectral_taps):
    n_cols = lax.axis_size("tx")
    ch = channel_cube.shape[0]
    channels = ch * lax.axis_size("ty") * n_cols
    packed = pack(channel_cube, footprint)
    own = lax.all_to_all(packed, ("ty", "tx"), split_axis=0, concat_axis=0, tiled=True)
    own = own.reshape(own.shape[0], GROUPS, ch, LANES)
    far_pairs = [(i, i + 1) for i in range(1, n_cols - 1, 2)]
    near_pairs = [(i, i + 1) for i in range(0, n_cols - 1, 2)]
    both = lambda pairs: pairs + [(j, i) for i, j in pairs]
    far, near = cut(own, True), cut(own, False)
    far = lax.ppermute(far, "tx", both(far_pairs))
    near = lax.ppermute(near, "tx", both(near_pairs))
    main, halo, *weights, box = tables(spectral_taps, channels)
    out, sums, scales = begin(
        kernel_sigmas, spectral_taps, footprint, own, near, main, halo, weights[: 2 * SMAX], box
    )
    return finish(kernel_sigmas, out, far, sums, scales, main, halo, weights[2 * SMAX :], box)


def solution(mesh):
    placed = (P(("ty", "tx"), None, None), P(), P(), P())
    return jax.shard_map(local, mesh=mesh, in_specs=placed, out_specs=P(None, "ty", "tx", None), check_vma=False)
```
